256 devices in a mesh: dp: 16 (over y, x_lo, core), space: 16 (over z, x_hi).
Axes of the slice: x: 4 (x_hi: 2, x_lo: 2; x = x_hi * 2 + x_lo), y: 4, z: 8, core: 2. Of those that a mesh axis runs over, the one named last changes fastest.
Arguments:
- images: bfloat16 [16, 64, 128, 1024], P('dp', 'space'), may hold values from -18 to 18
- teacher: bfloat16 [16, 64, 128, 1024], P('dp', 'space'), may hold values from 0 to 400
- w_reduce: bfloat16 [1024, 256], replicated, may hold values from -0.1875 to 0.1875
- w_spatial: bfloat16 [3, 3, 256, 256], replicated, may hold values from -0.125 to 0.125
- w_expand: bfloat16 [256, 1024], replicated, may hold values from -0.375 to 0.375
- partners: int32 [2, 16], replicated, may hold values from 0 to 15, as said below
Outputs:
- distill_loss: float32 [], replicated
- grad_images: bfloat16 [16, 64, 128, 1024], P('dp', 'space')
- grad_reduce: float32 [16, 1024, 256], P('dp', 'space')
- grad_spatial: float32 [16, 3, 3, 256, 256], P('dp', None, None, None, 'space')
- grad_expand: float32 [16, 256, 1024], P('dp', None, 'space')
The draws below stay inside these ranges and needn't reach their ends.
Inputs may be any that keep to these rules, and one draw needn't show every extreme that they name: partners[r, i] = i XOR m_r for a round value m_r of 1 to 15, the m_r distinct over rounds; so each round pairs the images and partners[r, partners[r, i]] = i.
All inputs are finite; a program needn't handle non-finite values.
Results may differ from the reference program's by a relative error of at most 0.019.
The reference program's roundings to bfloat16 on the way count: a program that leaves them out, or rounds other values in their place, can miss the bound.
Values may be sent and summed in bfloat16 or wider, within the bound.
No kernel may reach another device: no remote copies, remote signals or barrier semaphores. Data moves between devices by JAX's collectives and lax.ppermute only.
A program may use at most 64 MiB of HBM per device.

```python
import math
import jax
import jax.numpy as jnp
from jax import lax

C = 1024
MID = 256
COLS = 128
ROWS_DEV = 4
ROUNDS = 2
ROWS = 64
IMAGES = 16
ELEMS = 8388608


def draw_images(key, part):
    keys = jax.random.split(jax.random.fold_in(key, 5), 2)
    shape = (IMAGES, ROWS, COLS, C)
    base = jnp.clip(jax.random.normal(keys[0], shape, jnp.float32), -6.0, 6.0)
    band_count = ROWS // ROWS_DEV
    heavy = jax.random.randint(keys[1], (IMAGES, 1), 0, band_count).astype(jnp.int32)
    band_of_row = jnp.arange(ROWS, dtype=jnp.int32) // ROWS_DEV
    factor = jnp.where(band_of_row[None, :] == heavy, 3.0, 1.0).reshape(IMAGES, ROWS, 1, 1)
    return (base * factor).astype(jnp.bfloat16)


def draw_teacher(key, part):
    keys = jax.random.split(jax.random.fold_in(key, 11), 7)
    shape = (IMAGES, ROWS, COLS, C)
    noise = jnp.clip(jax.random.normal(keys[0], shape, jnp.float32), -6.0, 6.0) * 0.6
    common = jnp.clip(jax.random.normal(keys[4], (1, ROWS, COLS, C), jnp.float32), -4.0, 4.0)
    offset = jnp.clip(jax.random.normal(keys[1], (IMAGES, 1, 1, C), jnp.float32), -3.0, 3.0) * 0.5
    amount = jax.random.uniform(keys[5], (IMAGES, 1, 1, 1), jnp.float32, -2.0, 2.0)
    steps = (jnp.arange(COLS, dtype=jnp.float32) / max(COLS - 1, 1)).reshape(1, 1, COLS, 1)
    rising = jax.random.uniform(keys[6], (IMAGES, 1, 1, 1), jnp.float32) < 0.5
    ramp = jnp.exp(math.log(3.0) * jnp.where(rising, steps, 1.0 - steps))
    scale = jnp.exp(jax.random.uniform(keys[2], (1, 1, 1, C), jnp.float32) * math.log(10.0))
    band = jnp.exp(jax.random.uniform(keys[3], (IMAGES, ROWS, 1, 1), jnp.float32) * math.log(4.0))
    phase = jax.random.randint(jax.random.fold_in(key, 31), (IMAGES, 1, 1, 1), 0, 8).astype(jnp.int32)
    diag = (jnp.arange(ROWS, dtype=jnp.int32)[:, None] + jnp.arange(COLS, dtype=jnp.int32)[None, :]) % 8
    lattice = jnp.where(diag[None, :, :, None] == phase, 4.0, 1.0)
    values = lattice * scale * band * ramp * jax.nn.relu(offset + amount * common + noise)
    return jnp.clip(values, 0.0, 400.0).astype(jnp.bfloat16)


def draw_partners(key, part):
    order = jax.random.permutation(jax.random.fold_in(key, 23), IMAGES - 1)
    masks = order[:ROUNDS].astype(jnp.int32) + 1
    ranks = jnp.arange(IMAGES, dtype=jnp.int32)
    return jnp.bitwise_xor(ranks[None, :], masks[:, None]).astype(jnp.int32)


def centred(rng, shape, scale, reach, kind=jnp.bfloat16):
    values = jax.random.normal(rng, shape, jnp.float32) * scale
    return jnp.minimum(jnp.maximum(values, -reach), reach).astype(kind)


def setup_inputs(seed: int = 0) -> dict:
    key_of = jax.random.split(jax.random.key(seed), 7)
    return {
        "images": draw_images(jax.random.fold_in(key_of[6], 71), 0),
        "teacher": draw_teacher(jax.random.fold_in(key_of[6], 71), 0),
        "w_reduce": centred(key_of[2], (C, MID), C ** -0.5, 0.1875),
        "w_spatial": centred(key_of[3], (3, 3, MID, MID), (9 * MID) ** -0.5, 0.125),
        "w_expand": centred(key_of[4], (MID, C), MID ** -0.5, 0.375),
        "partners": draw_partners(jax.random.fold_in(key_of[6], 71), 0),
    }


def conv_taps(padded, weights, row_count, col_count, flipped):
    channels = padded.shape[-1]
    summed = None
    for row_step in range(3):
        for col_step in range(3):
            if flipped:
                window = padded[:, 2 - row_step:2 - row_step + row_count, 2 - col_step:2 - col_step + col_count, :]
                tap = weights[row_step, col_step].T
            else:
                window = padded[:, row_step:row_step + row_count, col_step:col_step + col_count, :]
                tap = weights[row_step, col_step]
            part_sum = jnp.dot(window.reshape(-1, channels), tap, preferred_element_type=jnp.float32)
            summed = part_sum if summed is None else summed + part_sum
    return summed

def gram_rows(features, partners):
    flat = features.reshape(features.shape[0], -1).astype(jnp.float32)
    columns = [lax.optimization_barrier(jnp.sum(flat * flat, axis=1))]
    for round_index in range(partners.shape[0]):
        columns.append(lax.optimization_barrier(jnp.sum(flat * flat[partners[round_index]], axis=1)))
    return jnp.stack(columns, axis=1)

def per_image(left, right, batch):
    left_img = left.reshape(batch, -1, left.shape[-1])
    right_img = right.reshape(batch, -1, right.shape[-1])
    return jnp.stack([jnp.dot(left_img[index].T, right_img[index], preferred_element_type=jnp.float32) for index in range(batch)])

def reference(images, teacher, w_reduce, w_spatial, w_expand, partners):
    batch, row_count, col_count, channels = images.shape
    hidden = w_reduce.shape[1]
    flat_x = images.reshape(-1, channels)
    h_one = jax.nn.relu(jnp.dot(flat_x, w_reduce, preferred_element_type=jnp.float32)).astype(jnp.bfloat16)
    pad_one = jnp.pad(h_one.reshape(batch, row_count, col_count, hidden), ((0, 0), (1, 1), (1, 1), (0, 0)))
    h_two = jax.nn.relu(conv_taps(pad_one, w_spatial, row_count, col_count, False)).astype(jnp.bfloat16)
    pre_act = jnp.dot(h_two, w_expand, preferred_element_type=jnp.float32) + flat_x.astype(jnp.float32)
    student = jax.nn.relu(pre_act).astype(jnp.bfloat16)
    student_img = student.reshape(batch, -1)
    v_student = gram_rows(student_img, partners)
    v_teacher = gram_rows(teacher.reshape(batch, -1), partners)
    nu_student = jnp.sqrt(lax.optimization_barrier(jnp.sum(v_student * v_student, axis=1, keepdims=True)) + 1e-06)
    nu_teacher = jnp.sqrt(lax.optimization_barrier(jnp.sum(v_teacher * v_teacher, axis=1, keepdims=True)) + 1e-06)
    n_student = v_student / nu_student
    n_teacher = v_teacher / nu_teacher
    diff = n_student - n_teacher
    distill_loss = jnp.sum(diff * diff)
    err = 2.0 * diff
    coefs = (err - lax.optimization_barrier(jnp.sum(err * n_student, axis=1, keepdims=True)) * n_student) / nu_student
    student_f = student_img.astype(jnp.float32)
    summed = 2.0 * coefs[:, 0:1] * student_f
    for round_index in range(partners.shape[0]):
        partner = partners[round_index]
        weight = coefs[:, round_index + 1] + coefs[partner, round_index + 1]
        summed = summed + weight[:, None] * student_f[partner]
    grad_student = (ELEMS * summed).astype(jnp.bfloat16).reshape(-1, channels)
    g_pre = jnp.where(student > 0, grad_student, jnp.zeros_like(grad_student))
    grad_expand = per_image(h_two, g_pre, batch)
    back_two = jnp.dot(g_pre, w_expand.T, preferred_element_type=jnp.float32)
    g_two = jnp.where(h_two > 0, back_two, 0.0).astype(jnp.bfloat16)
    g_two_img = g_two.reshape(batch, row_count, col_count, hidden)
    tap_grads = []
    for row_step in range(3):
        tap_row = []
        for col_step in range(3):
            window = pad_one[:, row_step:row_step + row_count, col_step:col_step + col_count, :].reshape(-1, hidden)
            tap_row.append(per_image(window, g_two, batch))
        tap_grads.append(jnp.stack(tap_row, axis=1))
    grad_spatial = jnp.stack(tap_grads, axis=1)
    pad_grad = jnp.pad(g_two_img, ((0, 0), (1, 1), (1, 1), (0, 0)))
    back_one = conv_taps(pad_grad, w_spatial, row_count, col_count, True)
    g_one = jnp.where(h_one > 0, back_one, 0.0).astype(jnp.bfloat16)
    grad_reduce = per_image(flat_x, g_one, batch)
    grad_images = (g_pre.astype(jnp.float32) + jnp.dot(g_one, w_reduce.T, preferred_element_type=jnp.float32)).astype(jnp.bfloat16)
    grad_images = grad_images.reshape(batch, row_count, col_count, channels)
    return (distill_loss, grad_images, grad_reduce, grad_spatial, grad_expand)
```

```python
import functools

import jax
import jax.numpy as jnp
from jax import lax
from jax.experimental import pallas as pl
from jax.experimental.pallas import tpu as pltpu
from jax.sharding import PartitionSpec as P

F32 = jnp.float32
BF16 = jnp.bfloat16
ROW_DOT = (((1,), (0,)), ((), ()))
LAST_DOT = (((1,), (1,)), ((), ()))
FIRST_DOT = (((0,), (0,)), ((), ()))


def dot(left, right, dims):
    return lax.dot_general(left, right, dims, preferred_element_type=F32)


def flat(value):
    return value.reshape(-1, value.shape[-1])


def shifted(value, step, cols):
    count = value.shape[0]
    moved = pltpu.roll(value, (-step) % count, 0)
    col = lax.broadcasted_iota(jnp.int32, value.shape, 0) % cols
    edge = cols - 1 if step == 1 else 0
    return jnp.where(col == edge, 0.0, moved)


def reduce_kernel(x_ref, w_ref, h_ref):
    acc = dot(x_ref[0], w_ref[...], ROW_DOT)
    h_ref[0] = jnp.maximum(acc, 0.0).astype(BF16)


def forward_kernel(
    h_ref, above_ref, below_ref, ws_ref, we_ref, x_ref, t_ref, hp_ref, h2_ref, st_ref
):
    rows, cols, mid = h_ref.shape
    devices, _, chunk, channels = st_ref.shape
    hp_ref[0] = above_ref[...]
    hp_ref[rows + 1] = below_ref[...]
    hp_ref[1 : rows + 1] = h_ref[...]
    sums = []
    for b in range(3):
        acc = None
        for a in range(3):
            part = dot(flat(hp_ref[a : a + rows]), ws_ref[a, b], ROW_DOT)
            acc = part if acc is None else acc + part
        sums.append(acc)
    total = sums[1] + shifted(sums[0], -1, cols) + shifted(sums[2], 1, cols)
    h_two = jnp.maximum(total, 0.0).astype(BF16)
    h2_ref[...] = h_two.reshape(rows, cols, mid)
    pre = dot(h_two, we_ref[...], ROW_DOT) + flat(x_ref[...]).astype(F32)
    st_ref[:, 0] = jnp.maximum(pre, 0.0).astype(BF16).reshape(devices, chunk, channels)
    st_ref[:, 1] = t_ref[...].reshape(devices, chunk, channels)


def gram_kernel(masks_ref, st_ref, out_ref):
    images, _, chunk, _ = st_ref.shape
    count = images * chunk
    row = lax.broadcasted_iota(jnp.int32, (count, count), 0)
    col = lax.broadcasted_iota(jnp.int32, (count, count), 1)
    same = (row % chunk) == (col % chunk)
    image = lax.broadcasted_iota(jnp.int32, (images, count), 0)
    other = lax.broadcasted_iota(jnp.int32, (images, count), 1) // chunk
    slot_row = lax.broadcasted_iota(jnp.int32, (images, 128), 0)
    slot = lax.broadcasted_iota(jnp.int32, (images, 128), 1)
    message = jnp.zeros((images, 128), F32)
    for which in range(2):
        value = flat(st_ref[:, which])
        gram = jnp.where(same, dot(value, value, LAST_DOT), 0.0)
        gram = gram.reshape(images, chunk, count).sum(axis=1)
        for k in range(3):
            partner = image if k == 0 else image ^ masks_ref[k - 1]
            column = jnp.where(other == partner, gram, 0.0).sum(axis=1, keepdims=True)
            message = message + jnp.where(slot == 8 * slot_row + 3 * which + k, column, 0.0)
    out_ref[...] = jnp.broadcast_to(message.sum(axis=0, keepdims=True), out_ref.shape)


def grad_kernel(scale, masks_ref, msg_ref, st_ref, g_ref, loss_ref):
    images = st_ref.shape[0]
    total = jnp.broadcast_to(msg_ref[...].sum(axis=0, keepdims=True), (images, 128))
    row = lax.broadcasted_iota(jnp.int32, (images, 128), 0)
    lane = lax.broadcasted_iota(jnp.int32, (images, 128), 1)

    def column(k):
        return jnp.where(lane == 8 * row + k, total, 0.0).sum(axis=1, keepdims=True)

    v_s = [column(k) for k in range(3)]
    v_t = [column(3 + k) for k in range(3)]
    nu_s = jnp.sqrt(v_s[0] * v_s[0] + v_s[1] * v_s[1] + v_s[2] * v_s[2] + 1e-06)
    nu_t = jnp.sqrt(v_t[0] * v_t[0] + v_t[1] * v_t[1] + v_t[2] * v_t[2] + 1e-06)
    n_s = [v / nu_s for v in v_s]
    diff = [a - b / nu_t for a, b in zip(n_s, v_t)]
    terms = diff[0] * diff[0] + diff[1] * diff[1] + diff[2] * diff[2]
    loss_ref[...] = terms.sum(axis=0, keepdims=True)
    err = [2.0 * d for d in diff]
    inner = err[0] * n_s[0] + err[1] * n_s[1] + err[2] * n_s[2]
    coefs = [(e - inner * n) / nu_s for e, n in zip(err, n_s)]
    weights = [2.0 * coefs[0]]
    for k in range(2):
        own = coefs[k + 1]
        as_row = jnp.where(row == lane, own, 0.0).sum(axis=0, keepdims=True)
        partner = row ^ masks_ref[k]
        theirs = jnp.where(lane == partner, as_row, 0.0).sum(axis=1, keepdims=True)
        weights.append(own + theirs)
    for i in range(images):
        own = st_ref[i, 0].astype(F32)
        acc = weights[0][i : i + 1] * own
        for k in range(2):
            acc = acc + weights[k + 1][i : i + 1] * st_ref[i ^ masks_ref[k], 0].astype(F32)
        g_ref[i] = jnp.where(own > 0.0, scale * acc, 0.0).astype(BF16)


def expand_kernel(g_ref, h2_ref, we_ref, g2_ref, ge_ref):
    grads = g_ref[...]
    h_two = flat(h2_ref[...])
    back = dot(grads, we_ref[...], LAST_DOT)
    g_two = jnp.where(h_two > 0, back, 0.0).astype(BF16)
    g2_ref[...] = g_two.reshape(g2_ref.shape)
    ge_ref[...] = dot(grads, h_two, FIRST_DOT).astype(BF16).reshape(ge_ref.shape)


def spatial_kernel(hp_ref, g2_ref, gs_ref):
    rows, cols, mid = g2_ref.shape
    chunks, _, _, width, _ = gs_ref.shape
    g_two = flat(g2_ref[...])
    wide = g_two.astype(F32)
    moved = [shifted(wide, 1, cols).astype(BF16), g_two, shifted(wide, -1, cols).astype(BF16)]
    for a in range(3):
        source = flat(hp_ref[a : a + rows])
        for b in range(3):
            part = dot(moved[b], source, FIRST_DOT).astype(BF16)
            gs_ref[:, a, b] = part.reshape(chunks, width, mid)


def backward_kernel(
    g2_ref, above_ref, below_ref, hp_ref, ws_ref, wr_ref, x_ref, g_ref, gr_ref, gi_ref, gp_ref
):
    rows, cols, mid = g2_ref.shape
    gp_ref[0] = above_ref[...]
    gp_ref[rows + 1] = below_ref[...]
    gp_ref[1 : rows + 1] = g2_ref[...]
    sums = []
    for b in range(3):
        acc = None
        for a in range(3):
            part = dot(flat(gp_ref[2 - a : 2 - a + rows]), ws_ref[a, b], LAST_DOT)
            acc = part if acc is None else acc + part
        sums.append(acc)
    total = sums[1] + shifted(sums[0], 1, cols) + shifted(sums[2], -1, cols)
    g_one = jnp.where(flat(hp_ref[1 : rows + 1]) > 0, total, 0.0).astype(BF16)
    gr_ref[...] = dot(flat(x_ref[...]), g_one, FIRST_DOT).astype(BF16).reshape(gr_ref.shape)
    back = dot(g_one, wr_ref[...], LAST_DOT)
    gi_ref[...] = (g_ref[...].astype(F32) + back).astype(BF16).reshape(gi_ref.shape)


def call(kernel, outs, smem=0, scratch=(), cost=None, name=None):
    def run(*args):
        return pl.pallas_call(
            kernel,
            out_shape=[jax.ShapeDtypeStruct(s, d) for s, d in outs],
            in_specs=[
                pl.BlockSpec(memory_space=pltpu.SMEM if i < smem else pltpu.VMEM)
                for i in range(len(args))
            ],
            out_specs=[pl.BlockSpec(memory_space=pltpu.VMEM) for _ in outs],
            scratch_shapes=list(scratch),
            compiler_params=pltpu.CompilerParams(vmem_limit_bytes=56 * 2**20),
            cost_estimate=cost,
            name=name,
        )(*args)

    return run


def cost(flops, nbytes):
    return pl.CostEstimate(flops=flops, bytes_accessed=nbytes, transcendentals=0)


def edges(value):
    peers = lax.axis_size("space")
    up = [(i, i + 1) for i in range(peers - 1)]
    down = [(i + 1, i) for i in range(peers - 1)]
    above = lax.ppermute(value[-1], "space", up)
    below = lax.ppermute(value[0], "space", down)
    return above, below


def scattered(local):
    peers = lax.axis_size("space")
    depth = peers // 2
    place = lax.axis_index("space")
    z, half = place // 2, place % 2
    ring_up = [(i, (i + 2) % peers) for i in range(peers)]
    ring_down = [(i, (i - 2) % peers) for i in range(peers)]

    def mine(block, side):
        return lax.dynamic_index_in_dim(local, 2 * (block % depth) + side, 0, keepdims=False)

    up = mine(z + depth - 1, 0)
    down = mine(z + 1, 1)
    for step in range(depth - 1):
        got_up = lax.ppermute(up, "space", ring_up)
        got_down = lax.ppermute(down, "space", ring_down)
        up = got_up.astype(F32) + mine(z + 2 * depth - 2 - step, 0).astype(F32)
        down = got_down.astype(F32) + mine(z + 2 + step, 1).astype(F32)
        if step < depth - 2:
            up, down = up.astype(BF16), down.astype(BF16)
    keep = jnp.where(half == 0, up, down)
    give = jnp.where(half == 0, down, up).astype(BF16)
    swap = [(i, i ^ 1) for i in range(peers)]
    return keep + lax.ppermute(give, "space", swap).astype(F32)


def body(images, teacher, w_reduce, w_spatial, w_expand, partners):
    _, rows, cols, channels = images.shape
    mid = w_reduce.shape[1]
    n_dp, n_space = lax.axis_size("dp"), lax.axis_size("space")
    pixels = rows * cols
    chunk = pixels // n_dp
    elems = float(rows * n_space * cols * channels)
    masks = partners[:, 0]
    x = images.reshape(rows, cols, channels)
    t = teacher.reshape(rows, cols, channels)

    h_one = pl.pallas_call(
        reduce_kernel,
        grid=(rows,),
        in_specs=[
            pl.BlockSpec((1, cols, channels), lambda r: (r, 0, 0)),
            pl.BlockSpec((channels, mid), lambda r: (0, 0)),
        ],
        out_specs=pl.BlockSpec((1, cols, mid), lambda r: (r, 0, 0)),
        out_shape=jax.ShapeDtypeStruct((rows, cols, mid), BF16),
        name="reduce",
    )(x, w_reduce)
    above, below = edges(h_one)
    h_pad, h_two, both = call(
        forward_kernel,
        [
            ((rows + 2, cols, mid), BF16),
            ((rows, cols, mid), BF16),
            ((n_dp, 2, chunk, channels), BF16),
        ],
        name="forward",
    )(h_one, above, below, w_spatial, w_expand, x, t)
    both = lax.all_to_all(both, "dp", 0, 0, tiled=True)
    world = n_dp * n_space
    (message,) = call(gram_kernel, [((world, 128), F32)], smem=1, name="gram")(masks, both)
    message = lax.all_to_all(message, ("dp", "space"), 0, 0, tiled=True)
    grads, loss = call(
        functools.partial(grad_kernel, elems),
        [((n_dp, chunk, channels), BF16), ((1, 1), F32)],
        smem=1,
        name="grad",
    )(masks, message, both)
    grads = lax.all_to_all(grads, "dp", 0, 0, tiled=True).reshape(pixels, channels)
    g_two, g_expand = call(
        expand_kernel,
        [((rows, cols, mid), BF16), ((n_space, channels // n_space, mid), BF16)],
        name="expand",
    )(grads, h_two, w_expand)
    above, below = edges(g_two)
    (g_spatial,) = call(
        spatial_kernel,
        [((n_space, 3, 3, mid // n_space, mid), BF16)],
        cost=cost(2 * 9 * pixels * mid * mid, 4 * pixels * mid),
        name="spatial",
    )(h_pad, g_two)
    g_reduce, g_images = call(
        backward_kernel,
        [((n_space, channels // n_space, mid), BF16), ((1, rows, cols, channels), BF16)],
        scratch=[pltpu.VMEM((rows + 2, cols, mid), BF16)],
        name="backward",
    )(g_two, above, below, h_pad, w_spatial, w_reduce, x, grads)
    part = channels // n_space
    local = jnp.concatenate(
        [g_expand, g_reduce, g_spatial.reshape(n_space, 9 * mid // n_space, mid)], axis=1
    )
    total = scattered(local)
    grad_expand = total[:part].T[None]
    grad_reduce = total[part : 2 * part][None]
    grad_spatial = total[2 * part :].reshape(3, 3, mid // n_space, mid).swapaxes(2, 3)[None]
    return loss[0, 0], g_images, grad_reduce, grad_spatial, grad_expand


def solution(mesh):
    return jax.shard_map(
        body,
        mesh=mesh,
        in_specs=(P("dp", "space", None, None), P("dp", "space", None, None), P(), P(), P(), P()),
        out_specs=(
            P(),
            P("dp", "space", None, None),
            P("dp", "space", None),
            P("dp", None, None, None, "space"),
            P("dp", None, "space"),
        ),
        check_vma=False,
    )
```

```python
import functools

import jax
import jax.numpy as jnp
from jax import lax
from jax.experimental import pallas as pl
from jax.experimental.pallas import tpu as pltpu
from jax.sharding import PartitionSpec as P

F32 = jnp.float32
BF16 = jnp.bfloat16
VMEM_LIMIT = 20 * 2**20
ROW_DOT = (((1,), (0,)), ((), ()))
LAST_DOT = (((1,), (1,)), ((), ()))
FIRST_DOT = (((0,), (0,)), ((), ()))


def dot(left, right, dims):
    return lax.dot_general(left, right, dims, preferred_element_type=F32)


def flat(value):
    return value.reshape(-1, value.shape[-1])


def shifted(value, step, cols):
    count = value.shape[0]
    moved = pltpu.roll(value, (-step) % count, 0)
    col = lax.broadcasted_iota(jnp.int32, value.shape, 0) % cols
    edge = cols - 1 if step == 1 else 0
    return jnp.where(col == edge, 0.0, moved)


def widened(parts, cols):
    return parts[1] + shifted(parts[0], -1, cols) + shifted(parts[2], 1, cols)


def narrowed(parts, cols):
    return parts[1] + shifted(parts[0], 1, cols) + shifted(parts[2], -1, cols)


def taps(sources, ws_ref, dims):
    sums = []
    for b in range(3):
        acc = None
        for a in range(3):
            part = dot(sources[a], ws_ref[a, b], dims)
            acc = part if acc is None else acc + part
        sums.append(acc)
    return sums


def edge_kernel(top_ref, end_ref, w_ref, first_ref, last_ref):
    for source, out in ((top_ref, first_ref), (end_ref, last_ref)):
        out[...] = jnp.maximum(dot(source[0], w_ref[...], ROW_DOT), 0.0).astype(BF16)


def inner_kernel(x_ref, wr_ref, first_ref, last_ref, ws_ref, we_ref, h_ref, h2_ref, s_ref):
    rows, cols, _ = h_ref.shape
    inside = rows - 2
    x_in = flat(x_ref[1 : rows - 1])
    h_in = jnp.maximum(dot(x_in, wr_ref[...], ROW_DOT), 0.0).astype(BF16)
    h_ref[0] = first_ref[...]
    h_ref[rows - 1] = last_ref[...]
    h_ref[1 : rows - 1] = h_in.reshape(inside, cols, -1)
    sums = taps([flat(h_ref[a : a + inside]) for a in range(3)], ws_ref, ROW_DOT)
    h_two = jnp.maximum(widened(sums, cols), 0.0).astype(BF16)
    h2_ref[...] = h_two
    pre = dot(h_two, we_ref[...], ROW_DOT) + x_in.astype(F32)
    s_ref[...] = jnp.maximum(pre, 0.0).astype(BF16).reshape(s_ref.shape)


def outer_kernel(h_ref, above_ref, below_ref, ws_ref, we_ref, x_ref, si_ref, h2_ref, s_ref):
    rows, cols, _ = h_ref.shape
    tops = [above_ref[...], h_ref[0], h_ref[1]]
    ends = [h_ref[rows - 2], h_ref[rows - 1], below_ref[...]]
    sources = [jnp.concatenate(pair, axis=0) for pair in zip(tops, ends)]
    h_two = jnp.maximum(widened(taps(sources, ws_ref, ROW_DOT), cols), 0.0).astype(BF16)
    h2_ref[...] = h_two
    x_out = jnp.concatenate([x_ref[0], x_ref[rows - 1]], axis=0)
    pre = dot(h_two, we_ref[...], ROW_DOT) + x_out.astype(F32)
    devices, split, channels = si_ref.shape
    s_ref[:, :split] = si_ref[...]
    s_ref[:, split:] = jnp.maximum(pre, 0.0).astype(BF16).reshape(devices, -1, channels)


def gram_kernel(base, parts_ref, *refs):
    value_ref, out_ref = refs[-2], refs[-1]
    images, chunk, _ = value_ref.shape
    count = images * chunk
    row = lax.broadcasted_iota(jnp.int32, (count, count), 0)
    col = lax.broadcasted_iota(jnp.int32, (count, count), 1)
    same = (row % chunk) == (col % chunk)
    image = lax.broadcasted_iota(jnp.int32, (images, count), 0)
    other = lax.broadcasted_iota(jnp.int32, (images, count), 1) // chunk
    slot_row = lax.broadcasted_iota(jnp.int32, (images, 128), 0)
    slot = lax.broadcasted_iota(jnp.int32, (images, 128), 1)
    message = jnp.zeros((images, 128), F32)
    value = flat(value_ref[...])
    gram = jnp.where(same, dot(value, value, LAST_DOT), 0.0)
    gram = gram.reshape(images, chunk, count).sum(axis=1)
    for k in range(3):
        partner = image if k == 0 else image ^ parts_ref[k - 1, 0]
        column = jnp.where(other == partner, gram, 0.0).sum(axis=1, keepdims=True)
        message = message + jnp.where(slot == 8 * slot_row + base + k, column, 0.0)
    total = message.sum(axis=0, keepdims=True)
    if len(refs) == 3:
        total = total + refs[0][...]
    out_ref[...] = jnp.broadcast_to(total, out_ref.shape)


def grad_kernel(scale, parts_ref, msg_ref, s_ref, g_ref, loss_ref):
    images = s_ref.shape[0]
    total = jnp.broadcast_to(msg_ref[...].sum(axis=0, keepdims=True), (images, 128))
    row = lax.broadcasted_iota(jnp.int32, (images, 128), 0)
    lane = lax.broadcasted_iota(jnp.int32, (images, 128), 1)

    def column(k):
        return jnp.where(lane == 8 * row + k, total, 0.0).sum(axis=1, keepdims=True)

    v_s = [column(k) for k in range(3)]
    v_t = [column(3 + k) for k in range(3)]
    nu_s = jnp.sqrt(v_s[0] * v_s[0] + v_s[1] * v_s[1] + v_s[2] * v_s[2] + 1e-06)
    nu_t = jnp.sqrt(v_t[0] * v_t[0] + v_t[1] * v_t[1] + v_t[2] * v_t[2] + 1e-06)
    n_s = [v / nu_s for v in v_s]
    diff = [a - b / nu_t for a, b in zip(n_s, v_t)]
    terms = diff[0] * diff[0] + diff[1] * diff[1] + diff[2] * diff[2]
    loss_ref[...] = terms.sum(axis=0, keepdims=True)
    err = [2.0 * d for d in diff]
    inner = err[0] * n_s[0] + err[1] * n_s[1] + err[2] * n_s[2]
    coefs = [(e - inner * n) / nu_s for e, n in zip(err, n_s)]
    weights = [2.0 * coefs[0]]
    for k in range(2):
        own = coefs[k + 1]
        as_row = jnp.where(row == lane, own, 0.0).sum(axis=0, keepdims=True)
        partner = row ^ parts_ref[k, 0]
        theirs = jnp.where(lane == partner, as_row, 0.0).sum(axis=1, keepdims=True)
        weights.append(own + theirs)
    for i in range(images):
        own = s_ref[i].astype(F32)
        acc = weights[0][i : i + 1] * own
        for k in range(2):
            acc = acc + weights[k + 1][i : i + 1] * s_ref[i ^ parts_ref[k, 0]].astype(F32)
        g_ref[i] = jnp.where(own > 0.0, scale * acc, 0.0).astype(BF16)


def halves(g_ref, h2i_ref):
    split = h2i_ref.shape[0] // g_ref.shape[0]
    return flat(g_ref[:, :split]), flat(g_ref[:, split:])


def back_kernel(g_ref, h2i_ref, h2o_ref, we_ref, g2_ref, first_ref, last_ref):
    rows, cols, _ = g2_ref.shape
    g_in, g_out = halves(g_ref, h2i_ref)
    back = dot(g_out, we_ref[...], LAST_DOT)
    g_two = jnp.where(h2o_ref[...] > 0, back, 0.0).astype(BF16)
    first_ref[...] = g_two[:cols]
    last_ref[...] = g_two[cols:]
    g2_ref[0] = g_two[:cols]
    g2_ref[rows - 1] = g_two[cols:]
    back = dot(g_in, we_ref[...], LAST_DOT)
    g_two = jnp.where(h2i_ref[...] > 0, back, 0.0).astype(BF16)
    g2_ref[1 : rows - 1] = g_two.reshape(rows - 2, cols, -1)


def window_kernel(
    g_ref, h2i_ref, h2o_ref, g2_ref, h_ref, above_ref, below_ref, ws_ref, out_ref, g1_ref, hp_ref
):
    rows, cols, mid = g2_ref.shape
    chunks = out_ref.shape[0]
    width = mid // chunks
    g_in, g_out = halves(g_ref, h2i_ref)
    expand = dot(g_in, h2i_ref[...], FIRST_DOT) + dot(g_out, h2o_ref[...], FIRST_DOT)
    part = expand.shape[0] // chunks
    out_ref[:, :part] = expand.astype(BF16).reshape(chunks, part, mid)
    hp_ref[0] = above_ref[...]
    hp_ref[rows + 1] = below_ref[...]
    hp_ref[1 : rows + 1] = h_ref[...]
    g_two = flat(g2_ref[...])
    wide = g_two.astype(F32)
    moved = [shifted(wide, 1, cols).astype(BF16), g_two, shifted(wide, -1, cols).astype(BF16)]
    for a in range(3):
        source = flat(hp_ref[a : a + rows])
        for b in range(3):
            start = part + (3 * a + b) * width
            grad = dot(moved[b], source, FIRST_DOT).astype(BF16)
            out_ref[:, start : start + width] = grad.reshape(chunks, width, mid)
    inside = rows - 2
    sums = taps([flat(g2_ref[2 - a : 2 - a + inside]) for a in range(3)], ws_ref, LAST_DOT)
    total = narrowed(sums, cols)
    g1_ref[...] = jnp.where(flat(h_ref[1 : rows - 1]) > 0, total, 0.0).astype(BF16)


def backward_kernel(
    g2_ref, above_ref, below_ref, h_ref, ws_ref, x_ref, g1i_ref, out_ref, g1o_ref
):
    rows = g2_ref.shape[0]
    cols = g2_ref.shape[1]
    tops = [g2_ref[1], g2_ref[0], above_ref[...]]
    ends = [below_ref[...], g2_ref[rows - 1], g2_ref[rows - 2]]
    sources = [jnp.concatenate(pair, axis=0) for pair in zip(tops, ends)]
    total = narrowed(taps(sources, ws_ref, LAST_DOT), cols)
    h_out = jnp.concatenate([h_ref[0], h_ref[rows - 1]], axis=0)
    g_one = jnp.where(h_out > 0, total, 0.0).astype(BF16)
    g1o_ref[...] = g_one
    x_out = jnp.concatenate([x_ref[0], x_ref[rows - 1]], axis=0)
    grad = dot(x_out, g_one, FIRST_DOT) + dot(flat(x_ref[1 : rows - 1]), g1i_ref[...], FIRST_DOT)
    out_ref[...] = grad.astype(BF16).reshape(out_ref.shape)


def images_kernel(g_ref, g1i_ref, g1o_ref, wr_ref, out_ref):
    _, rows, cols, _ = out_ref.shape
    g_in, g_out = halves(g_ref, g1i_ref)
    inner = (g_in.astype(F32) + dot(g1i_ref[...], wr_ref[...], LAST_DOT)).astype(BF16)
    outer = (g_out.astype(F32) + dot(g1o_ref[...], wr_ref[...], LAST_DOT)).astype(BF16)
    out_ref[0, 0] = outer[:cols]
    out_ref[0, rows - 1] = outer[cols:]
    out_ref[0, 1 : rows - 1] = inner.reshape(rows - 2, cols, -1)


def call(kernel, outs, flops, smem=0, scratch=()):
    def run(*args):
        specs = [
            pl.BlockSpec(memory_space=pltpu.SMEM if i < smem else pltpu.VMEM)
            for i in range(len(args))
        ]
        moved = sum(v.size * v.dtype.itemsize for v in args)
        return pl.pallas_call(
            kernel,
            out_shape=[jax.ShapeDtypeStruct(s, d) for s, d in outs],
            in_specs=specs,
            out_specs=[pl.BlockSpec(memory_space=pltpu.VMEM) for _ in outs],
            scratch_shapes=list(scratch),
            compiler_params=pltpu.CompilerParams(vmem_limit_bytes=VMEM_LIMIT),
            cost_estimate=pl.CostEstimate(flops=flops, bytes_accessed=moved, transcendentals=0),
        )(*args)

    return run


def exchanged(first, last):
    peers = lax.axis_size("space")
    up = [(i, i + 1) for i in range(peers - 1)]
    down = [(i + 1, i) for i in range(peers - 1)]
    return lax.ppermute(last, "space", up), lax.ppermute(first, "space", down)


def scattered(local):
    peers = lax.axis_size("space")
    depth, (_, rows, mid) = peers // 2, local.shape
    far = depth // 2
    place = lax.axis_index("space")
    z, half = place // 2, place % 2
    ring_up = [(i, (i + 2) % peers) for i in range(peers)]
    ring_down = [(i, (i - 2) % peers) for i in range(peers)]
    pairs = local.reshape(depth, 2, rows, mid)

    def mine(block):
        return lax.dynamic_index_in_dim(pairs, block % depth, 0, keepdims=False)

    start = mine(z + far)
    up, down = start[0], start[1]
    for step in range(1, far + 1):
        got_up = lax.ppermute(up, "space", ring_up)
        got_down = lax.ppermute(down, "space", ring_down)
        got_up, got_down = lax.optimization_barrier((got_up, got_down))
        got_up, got_down = got_up.astype(F32), got_down.astype(F32)
        if step == 1:
            got_up = jnp.stack([got_up, jnp.zeros_like(got_up)])
            got_down = jnp.stack([jnp.zeros_like(got_down), got_down])
        if step < far:
            up = (mine(z + far - step).astype(F32) + got_up).astype(BF16)
            down = (mine(z - far + step + depth).astype(F32) + got_down).astype(BF16)
    total = mine(z).astype(F32) + got_up + got_down
    keep = jnp.where(half == 0, total[0], total[1])
    give = jnp.where(half == 0, total[1], total[0]).astype(BF16)
    swap = [(i, i ^ 1) for i in range(peers)]
    return keep + lax.ppermute(give, "space", swap).astype(F32)


def step(images, teacher, w_reduce, w_spatial, w_expand, partners):
    _, rows, cols, channels = images.shape
    mid = w_reduce.shape[1]
    n_dp, n_space = lax.axis_size("dp"), lax.axis_size("space")
    pixels = rows * cols
    chunk = pixels // n_dp
    inside, outside = (rows - 2) * cols, 2 * cols
    split = inside // n_dp
    elems = float(pixels * n_space * channels)
    world = n_dp * n_space
    x = images.reshape(rows, cols, channels)

    t_all = lax.all_to_all(teacher.reshape(n_dp, chunk, channels), "dp", 0, 0, tiled=True)
    first, last = pl.pallas_call(
        edge_kernel,
        grid=(1,),
        in_specs=[
            pl.BlockSpec((1, cols, channels), lambda i: (0, 0, 0)),
            pl.BlockSpec((1, cols, channels), lambda i: (rows - 1, 0, 0)),
            pl.BlockSpec((channels, mid), lambda i: (0, 0)),
        ],
        out_specs=[pl.BlockSpec((cols, mid), lambda i: (0, 0))] * 2,
        out_shape=[jax.ShapeDtypeStruct((cols, mid), BF16)] * 2,
        compiler_params=pltpu.CompilerParams(vmem_limit_bytes=VMEM_LIMIT),
        name="edge",
    )(x, x, w_reduce)
    above, below = exchanged(first, last)
    mac = 2 * cols * mid * mid
    h_one, h_in, s_in = call(
        inner_kernel,
        [
            ((rows, cols, mid), BF16),
            ((inside, mid), BF16),
            ((n_dp, split, channels), BF16),
        ],
        26 * mac,
    )(x, w_reduce, first, last, w_spatial, w_expand)
    h_out, s_all = call(
        outer_kernel, [((outside, mid), BF16), ((n_dp, chunk, channels), BF16)], 26 * mac
    )(h_one, above, below, w_spatial, w_expand, x, s_in)
    s_all = lax.all_to_all(s_all, "dp", 0, 0, tiled=True)

    def gram(base, shape, flops):
        kernel = functools.partial(gram_kernel, base)
        return call(kernel, [(shape, F32)], flops, smem=1)

    (message,) = gram(3, (1, 128), 16 * mac)(partners, t_all)
    (message,) = gram(0, (world, 128), 16 * mac)(partners, message, s_all)
    message = lax.all_to_all(message, ("dp", "space"), 0, 0, tiled=True)
    grads, loss = call(
        functools.partial(grad_kernel, elems),
        [((n_dp, chunk, channels), BF16), ((1, 1), F32)],
        mac,
        smem=1,
    )(partners, message, s_all)
    grads = lax.all_to_all(grads, "dp", 0, 0, tiled=True)
    g_two, first, last = call(
        back_kernel, [((rows, cols, mid), BF16), ((cols, mid), BF16), ((cols, mid), BF16)], 16 * mac
    )(grads, h_in, h_out, w_expand)
    over, under = exchanged(first, last)
    part, width = channels // n_space, mid // n_space
    early, g1_in = call(
        window_kernel,
        [((n_space, part + 9 * width, mid), BF16), ((inside, mid), BF16)],
        70 * mac,
        scratch=[pltpu.VMEM((rows + 2, cols, mid), BF16)],
    )(grads, h_in, h_out, g_two, h_one, above, below, w_spatial)
    late, g1_out = call(
        backward_kernel, [((n_space, part, mid), BF16), ((outside, mid), BF16)], 34 * mac
    )(g_two, over, under, h_one, w_spatial, x, g1_in)
    (g_images,) = call(
        images_kernel, [((1, rows, cols, channels), BF16)], 16 * mac
    )(grads, g1_in, g1_out, w_reduce)
    early, late = scattered(early), scattered(late)
    grad_expand = early[:part].T[None]
    grad_reduce = late[None]
    grad_spatial = early[part:].reshape(3, 3, width, mid).swapaxes(2, 3)[None]
    return loss[0, 0], g_images, grad_reduce, grad_spatial, grad_expand


def solution(mesh):
    return jax.shard_map(
        step,
        mesh=mesh,
        in_specs=(P("dp", "space", None, None), P("dp", "space", None, None), P(), P(), P(), P()),
        out_specs=(
            P(),
            P("dp", "space", None, None),
            P("dp", "space", None),
            P("dp", None, None, None, "space"),
            P("dp", None, "space"),
        ),
        check_vma=False,
    )
```

```python
import functools

import jax
import jax.numpy as jnp
from jax import lax
from jax.experimental import pallas as pl
from jax.experimental.pallas import tpu as pltpu
from jax.sharding import PartitionSpec as P

F32 = jnp.float32
BF16 = jnp.bfloat16
VMEM_LIMIT = 20 * 2**20
ROW_DOT = (((1,), (0,)), ((), ()))
LAST_DOT = (((1,), (1,)), ((), ()))
FIRST_DOT = (((0,), (0,)), ((), ()))


def dot(left, right, dims):
    return lax.dot_general(left, right, dims, preferred_element_type=F32)


def flat(value):
    return value.reshape(-1, value.shape[-1])


def shifted(value, step, cols):
    count = value.shape[0]
    moved = pltpu.roll(value, (-step) % count, 0)
    col = lax.broadcasted_iota(jnp.int32, value.shape, 0) % cols
    edge = cols - 1 if step == 1 else 0
    return jnp.where(col == edge, 0.0, moved)


def widened(parts, cols):
    return parts[1] + shifted(parts[0], -1, cols) + shifted(parts[2], 1, cols)


def narrowed(parts, cols):
    return parts[1] + shifted(parts[0], 1, cols) + shifted(parts[2], -1, cols)


def taps(sources, ws_ref, dims):
    sums = []
    for b in range(3):
        acc = None
        for a in range(3):
            part = dot(sources[a], ws_ref[a, b], dims)
            acc = part if acc is None else acc + part
        sums.append(acc)
    return sums


def edge_kernel(top_ref, end_ref, w_ref, first_ref, last_ref):
    for source, out in ((top_ref, first_ref), (end_ref, last_ref)):
        out[...] = jnp.maximum(dot(source[0], w_ref[...], ROW_DOT), 0.0).astype(BF16)


def inner_kernel(x_ref, wr_ref, first_ref, last_ref, ws_ref, we_ref, h_ref, h2_ref, s_ref):
    rows, cols, _ = h_ref.shape
    inside = rows - 2
    x_in = flat(x_ref[1 : rows - 1])
    h_in = jnp.maximum(dot(x_in, wr_ref[...], ROW_DOT), 0.0).astype(BF16)
    h_ref[0] = first_ref[...]
    h_ref[rows - 1] = last_ref[...]
    h_ref[1 : rows - 1] = h_in.reshape(inside, cols, -1)
    sums = taps([flat(h_ref[a : a + inside]) for a in range(3)], ws_ref, ROW_DOT)
    h_two = jnp.maximum(widened(sums, cols), 0.0).astype(BF16)
    h2_ref[...] = h_two
    pre = dot(h_two, we_ref[...], ROW_DOT) + x_in.astype(F32)
    s_ref[...] = jnp.maximum(pre, 0.0).astype(BF16).reshape(s_ref.shape)


def outer_kernel(
    h_ref, h2i_ref, above_ref, below_ref, ws_ref, we_ref, x_ref, si_ref, hp_ref, h2_ref, s_ref
):
    rows, cols, _ = h_ref.shape
    devices, split, channels = si_ref.shape
    inside = h2i_ref.shape[0]
    s_ref[:, :split] = si_ref[...]
    hp_ref[0] = above_ref[...]
    hp_ref[1 : rows + 1] = h_ref[...]
    hp_ref[rows + 1] = below_ref[...]
    tops = [above_ref[...], h_ref[0], h_ref[1]]
    ends = [h_ref[rows - 2], h_ref[rows - 1], below_ref[...]]
    sources = [jnp.concatenate(pair, axis=0) for pair in zip(tops, ends)]
    h_two = jnp.maximum(widened(taps(sources, ws_ref, ROW_DOT), cols), 0.0).astype(BF16)
    h2_ref[:inside] = h2i_ref[...]
    h2_ref[inside:] = h_two
    x_out = jnp.concatenate([x_ref[0], x_ref[rows - 1]], axis=0)
    pre = dot(h_two, we_ref[...], ROW_DOT) + x_out.astype(F32)
    s_ref[:, split:] = jnp.maximum(pre, 0.0).astype(BF16).reshape(devices, -1, channels)


def gram_kernel(parts_ref, s_ref, t_ref, out_ref):
    images, chunk, _ = s_ref.shape
    count = images * chunk
    row = lax.broadcasted_iota(jnp.int32, (count, count), 0)
    col = lax.broadcasted_iota(jnp.int32, (count, count), 1)
    same = (row % chunk) == (col % chunk)
    image = lax.broadcasted_iota(jnp.int32, (images, count), 0)
    other = lax.broadcasted_iota(jnp.int32, (images, count), 1) // chunk
    slot_row = lax.broadcasted_iota(jnp.int32, (images, 128), 0)
    slot = lax.broadcasted_iota(jnp.int32, (images, 128), 1)
    message = jnp.zeros((images, 128), F32)
    for base, value_ref in ((0, s_ref), (3, t_ref)):
        value = flat(value_ref[...])
        gram = jnp.where(same, dot(value, value, LAST_DOT), 0.0)
        gram = gram.reshape(images, chunk, count).sum(axis=1)
        for k in range(3):
            partner = image if k == 0 else image ^ parts_ref[k - 1, 0]
            column = jnp.where(other == partner, gram, 0.0).sum(axis=1, keepdims=True)
            message = message + jnp.where(slot == 8 * slot_row + base + k, column, 0.0)
    out_ref[...] = jnp.broadcast_to(message.sum(axis=0, keepdims=True), out_ref.shape)


def grad_kernel(scale, parts_ref, msg_ref, s_ref, g_ref, loss_ref):
    images = s_ref.shape[0]
    total = jnp.broadcast_to(msg_ref[...].sum(axis=0, keepdims=True), (images, 128))
    row = lax.broadcasted_iota(jnp.int32, (images, 128), 0)
    lane = lax.broadcasted_iota(jnp.int32, (images, 128), 1)

    def column(k):
        return jnp.where(lane == 8 * row + k, total, 0.0).sum(axis=1, keepdims=True)

    v_s = [column(k) for k in range(3)]
    v_t = [column(3 + k) for k in range(3)]
    nu_s = jnp.sqrt(v_s[0] * v_s[0] + v_s[1] * v_s[1] + v_s[2] * v_s[2] + 1e-06)
    nu_t = jnp.sqrt(v_t[0] * v_t[0] + v_t[1] * v_t[1] + v_t[2] * v_t[2] + 1e-06)
    n_s = [v / nu_s for v in v_s]
    diff = [a - b / nu_t for a, b in zip(n_s, v_t)]
    terms = diff[0] * diff[0] + diff[1] * diff[1] + diff[2] * diff[2]
    loss_ref[...] = terms.sum(axis=0, keepdims=True)
    err = [2.0 * d for d in diff]
    inner = err[0] * n_s[0] + err[1] * n_s[1] + err[2] * n_s[2]
    coefs = [(e - inner * n) / nu_s for e, n in zip(err, n_s)]
    weights = [2.0 * coefs[0]]
    for k in range(2):
        own = coefs[k + 1]
        as_row = jnp.where(row == lane, own, 0.0).sum(axis=0, keepdims=True)
        partner = row ^ parts_ref[k, 0]
        theirs = jnp.where(lane == partner, as_row, 0.0).sum(axis=1, keepdims=True)
        weights.append(own + theirs)
    for i in range(images):
        own = s_ref[i].astype(F32)
        acc = weights[0][i : i + 1] * own
        for k in range(2):
            acc = acc + weights[k + 1][i : i + 1] * s_ref[i ^ parts_ref[k, 0]].astype(F32)
        g_ref[i] = jnp.where(own > 0.0, scale * acc, 0.0).astype(BF16)


def halves(g_ref, inside):
    split = inside // g_ref.shape[0]
    return flat(g_ref[:, :split]), flat(g_ref[:, split:])


def back_kernel(g_ref, h2_ref, we_ref, g2_ref, first_ref, last_ref):
    rows, cols, _ = g2_ref.shape
    inside = (rows - 2) * cols
    g_in, g_out = halves(g_ref, inside)
    back = dot(g_out, we_ref[...], LAST_DOT)
    g_two = jnp.where(h2_ref[inside:] > 0, back, 0.0).astype(BF16)
    first_ref[...] = g_two[:cols]
    last_ref[...] = g_two[cols:]
    g2_ref[0] = g_two[:cols]
    g2_ref[rows - 1] = g_two[cols:]
    back = dot(g_in, we_ref[...], LAST_DOT)
    g_two = jnp.where(h2_ref[:inside] > 0, back, 0.0).astype(BF16)
    g2_ref[1 : rows - 1] = g_two.reshape(rows - 2, cols, -1)


def farthest(place_ref, local_ref, up_ref, down_ref):
    depth = local_ref.shape[0] // 2
    block = 2 * ((place_ref[0] // 2 + depth // 2) % depth)
    up_ref[...] = local_ref[block]
    down_ref[...] = local_ref[block + 1]


def window_kernel(
    place_ref, g_ref, h2_ref, g2_ref, hp_ref, ws_ref, out_ref, g1_ref, up_ref, down_ref
):
    rows, cols, mid = g2_ref.shape
    chunks = out_ref.shape[0]
    width = mid // chunks
    inside = (rows - 2) * cols
    g_in, g_out = halves(g_ref, inside)
    expand = dot(g_in, h2_ref[:inside], FIRST_DOT) + dot(g_out, h2_ref[inside:], FIRST_DOT)
    part = expand.shape[0] // chunks
    out_ref[:, :part] = expand.astype(BF16).reshape(chunks, part, mid)
    g_two = flat(g2_ref[...])
    wide = g_two.astype(F32)
    moved = [shifted(wide, 1, cols).astype(BF16), g_two, shifted(wide, -1, cols).astype(BF16)]
    for a in range(3):
        source = flat(hp_ref[a : a + rows])
        for b in range(3):
            start = part + (3 * a + b) * width
            grad = dot(moved[b], source, FIRST_DOT).astype(BF16)
            out_ref[:, start : start + width] = grad.reshape(chunks, width, mid)
    farthest(place_ref, out_ref, up_ref, down_ref)
    sums = taps([flat(g2_ref[2 - a : rows - a]) for a in range(3)], ws_ref, LAST_DOT)
    total = narrowed(sums, cols)
    g1_ref[...] = jnp.where(flat(hp_ref[2:rows]) > 0, total, 0.0).astype(BF16)


def backward_kernel(
    place_ref, g2_ref, above_ref, below_ref, hp_ref, ws_ref, x_ref, g1i_ref,
    out_ref, g1o_ref, up_ref, down_ref,
):
    rows = g2_ref.shape[0]
    cols = g2_ref.shape[1]
    tops = [g2_ref[1], g2_ref[0], above_ref[...]]
    ends = [below_ref[...], g2_ref[rows - 1], g2_ref[rows - 2]]
    sources = [jnp.concatenate(pair, axis=0) for pair in zip(tops, ends)]
    total = narrowed(taps(sources, ws_ref, LAST_DOT), cols)
    h_out = jnp.concatenate([hp_ref[1], hp_ref[rows]], axis=0)
    g_one = jnp.where(h_out > 0, total, 0.0).astype(BF16)
    g1o_ref[...] = g_one
    x_out = jnp.concatenate([x_ref[0], x_ref[rows - 1]], axis=0)
    grad = dot(x_out, g_one, FIRST_DOT) + dot(flat(x_ref[1 : rows - 1]), g1i_ref[...], FIRST_DOT)
    out_ref[...] = grad.astype(BF16).reshape(out_ref.shape)
    farthest(place_ref, out_ref, up_ref, down_ref)


def images_kernel(g_ref, g1i_ref, g1o_ref, wr_ref, out_ref):
    _, rows, cols, _ = out_ref.shape
    g_in, g_out = halves(g_ref, g1i_ref.shape[0])
    inner = (g_in.astype(F32) + dot(g1i_ref[...], wr_ref[...], LAST_DOT)).astype(BF16)
    outer = (g_out.astype(F32) + dot(g1o_ref[...], wr_ref[...], LAST_DOT)).astype(BF16)
    out_ref[0, 0] = outer[:cols]
    out_ref[0, rows - 1] = outer[cols:]
    out_ref[0, 1 : rows - 1] = inner.reshape(rows - 2, cols, -1)


def local_blocks(place_ref, offset, early_ref, late_ref):
    depth = early_ref.shape[0] // 2
    block = 2 * ((place_ref[0] // 2 + offset + depth) % depth)
    pairs = []
    for side in range(2):
        pairs.append(
            (early_ref[block + side].astype(F32), late_ref[block + side].astype(F32))
        )
    return pairs


def join_kernel(offset, place_ref, early_ref, late_ref, eu, ed, lu, ld, up_ref, down_ref):
    rows = early_ref.shape[1]
    for side_got, sign, got, out_ref in ((0, 1, (eu, lu), up_ref), (1, -1, (ed, ld), down_ref)):
        pairs = local_blocks(place_ref, sign * offset, early_ref, late_ref)
        for side, (early, late) in enumerate(pairs):
            if side == side_got:
                early, late = early + got[0][...].astype(F32), late + got[1][...].astype(F32)
            out_ref[side, :rows] = early.astype(BF16)
            out_ref[side, rows:] = late.astype(BF16)


def pass_kernel(offset, place_ref, early_ref, late_ref, gu_ref, gd_ref, up_ref, down_ref):
    rows = early_ref.shape[1]
    for sign, got_ref, out_ref in ((1, gu_ref, up_ref), (-1, gd_ref, down_ref)):
        pairs = local_blocks(place_ref, sign * offset, early_ref, late_ref)
        for side, (early, late) in enumerate(pairs):
            out_ref[side, :rows] = (early + got_ref[side, :rows].astype(F32)).astype(BF16)
            out_ref[side, rows:] = (late + got_ref[side, rows:].astype(F32)).astype(BF16)


def close_kernel(place_ref, early_ref, late_ref, gu_ref, gd_ref, keep_ref, give_ref):
    rows = early_ref.shape[1]
    half = place_ref[0] % 2
    for ref, side in ((keep_ref, half), (give_ref, 1 - half)):
        block = 2 * (place_ref[0] // 2) + side
        for local_ref, place in ((early_ref, slice(0, rows)), (late_ref, slice(rows, None))):
            total = local_ref[block].astype(F32) + gu_ref[side, place].astype(F32)
            total = total + gd_ref[side, place].astype(F32)
            ref[place] = total.astype(ref.dtype)


def last_kernel(keep_ref, got_ref, expand_ref, spatial_ref, reduce_ref):
    total = keep_ref[...] + got_ref[...].astype(F32)
    part, own = expand_ref.shape[0], reduce_ref.shape[0]
    expand_ref[...] = total[:part]
    spatial_ref[...] = total[part:-own].reshape(spatial_ref.shape)
    reduce_ref[...] = total[-own:]


def call(kernel, outs, flops, smem=0, scratch=()):
    def run(*args):
        specs = [
            pl.BlockSpec(memory_space=pltpu.SMEM if i < smem else pltpu.VMEM)
            for i in range(len(args))
        ]
        moved = sum(v.size * v.dtype.itemsize for v in args)
        return pl.pallas_call(
            kernel,
            out_shape=[jax.ShapeDtypeStruct(s, d) for s, d in outs],
            in_specs=specs,
            out_specs=[pl.BlockSpec(memory_space=pltpu.VMEM) for _ in outs],
            scratch_shapes=list(scratch),
            compiler_params=pltpu.CompilerParams(vmem_limit_bytes=VMEM_LIMIT),
            cost_estimate=pl.CostEstimate(flops=flops, bytes_accessed=moved, transcendentals=0),
        )(*args)

    return run


def exchanged(first, last):
    peers = lax.axis_size("space")
    up = [(i, i + 1) for i in range(peers - 1)]
    down = [(i + 1, i) for i in range(peers - 1)]
    return lax.ppermute(last, "space", up), lax.ppermute(first, "space", down)


def scattered(early, late, early_sends, late_sends, place):
    peers = lax.axis_size("space")
    far = peers // 4
    ring_up = [(i, (i + 2) % peers) for i in range(peers)]
    ring_down = [(i, (i - 2) % peers) for i in range(peers)]
    rows, mid = early.shape[1] + late.shape[1], early.shape[2]
    pair = [((2, rows, mid), BF16)] * 2

    def moved(up, down):
        up = lax.ppermute(up, "space", ring_up)
        down = lax.ppermute(down, "space", ring_down)
        return up, down

    got = moved(*early_sends) + moved(*late_sends)
    for step in range(2, far + 1):
        kernel = join_kernel if step == 2 else pass_kernel
        kernel = functools.partial(kernel, far + 1 - step)
        got = call(kernel, pair, rows * mid, smem=1)(place, early, late, *got)
        got = moved(*got)
    outs = [((rows, mid), F32), ((rows, mid), BF16)]
    keep, give = call(close_kernel, outs, rows * mid, smem=1)(place, early, late, *got)
    swap = [(i, i ^ 1) for i in range(peers)]
    return keep, lax.ppermute(give, "space", swap)


def step(images, teacher, w_reduce, w_spatial, w_expand, partners):
    _, rows, cols, channels = images.shape
    mid = w_reduce.shape[1]
    n_dp, n_space = lax.axis_size("dp"), lax.axis_size("space")
    pixels = rows * cols
    chunk = pixels // n_dp
    inside, outside = (rows - 2) * cols, 2 * cols
    split = inside // n_dp
    elems = float(pixels * n_space * channels)
    world = n_dp * n_space
    x = images.reshape(rows, cols, channels)
    place = lax.axis_index("space").reshape(1)
    teacher, place = lax.optimization_barrier((teacher, place))

    t_all = lax.all_to_all(teacher.reshape(n_dp, chunk, channels), "dp", 0, 0, tiled=True)
    first, last = pl.pallas_call(
        edge_kernel,
        grid=(1,),
        in_specs=[
            pl.BlockSpec((1, cols, channels), lambda i: (0, 0, 0)),
            pl.BlockSpec((1, cols, channels), lambda i: (rows - 1, 0, 0)),
            pl.BlockSpec((channels, mid), lambda i: (0, 0)),
        ],
        out_specs=[pl.BlockSpec((cols, mid), lambda i: (0, 0))] * 2,
        out_shape=[jax.ShapeDtypeStruct((cols, mid), BF16)] * 2,
        compiler_params=pltpu.CompilerParams(vmem_limit_bytes=VMEM_LIMIT),
        name="edge",
    )(x, x, w_reduce)
    above, below = exchanged(first, last)
    mac = 2 * cols * mid * mid
    h_one, h_in, s_in = call(
        inner_kernel,
        [
            ((rows, cols, mid), BF16),
            ((inside, mid), BF16),
            ((n_dp, split, channels), BF16),
        ],
        26 * mac,
    )(x, w_reduce, first, last, w_spatial, w_expand)
    h_pad, h_two, s_all = call(
        outer_kernel,
        [
            ((rows + 2, cols, mid), BF16),
            ((pixels, mid), BF16),
            ((n_dp, chunk, channels), BF16),
        ],
        26 * mac,
    )(h_one, h_in, above, below, w_spatial, w_expand, x, s_in)
    s_all = lax.all_to_all(s_all, "dp", 0, 0, tiled=True)

    (message,) = call(gram_kernel, [((world, 128), F32)], 32 * mac, smem=1)(partners, s_all, t_all)
    message = lax.all_to_all(message, ("dp", "space"), 0, 0, tiled=True)
    grads, loss = call(
        functools.partial(grad_kernel, elems),
        [((n_dp, chunk, channels), BF16), ((1, 1), F32)],
        mac,
        smem=1,
    )(partners, message, s_all)
    grads = lax.all_to_all(grads, "dp", 0, 0, tiled=True)
    g_two, first, last = call(
        back_kernel, [((rows, cols, mid), BF16), ((cols, mid), BF16), ((cols, mid), BF16)], 16 * mac
    )(grads, h_two, w_expand)
    over, under = exchanged(first, last)
    part, width = channels // n_space, mid // n_space
    early, g1_in, *early_sends = call(
        window_kernel,
        [((n_space, part + 9 * width, mid), BF16), ((inside, mid), BF16)]
        + [((part + 9 * width, mid), BF16)] * 2,
        70 * mac,
        smem=1,
    )(place, grads, h_two, g_two, h_pad, w_spatial)
    late, g1_out, *late_sends = call(
        backward_kernel,
        [((n_space, part, mid), BF16), ((outside, mid), BF16)] + [((part, mid), BF16)] * 2,
        34 * mac,
        smem=1,
    )(place, g_two, over, under, h_pad, w_spatial, x, g1_in)
    (g_images,) = call(
        images_kernel, [((1, rows, cols, channels), BF16)], 16 * mac
    )(grads, g1_in, g1_out, w_reduce)
    g_expand, g_spatial, g_reduce = call(
        last_kernel, [((part, mid), F32), ((3, 3, width, mid), F32), ((part, mid), F32)], mac
    )(*scattered(early, late, early_sends, late_sends, place))
    return (
        loss[0, 0],
        g_images,
        g_reduce[None],
        g_spatial.swapaxes(2, 3)[None],
        g_expand.T[None],
    )


def solution(mesh):
    return jax.shard_map(
        step,
        mesh=mesh,
        in_specs=(P("dp", "space", None, None), P("dp", "space", None, None), P(), P(), P(), P()),
        out_specs=(
            P(),
            P("dp", "space", None, None),
            P("dp", "space", None),
            P("dp", None, None, None, "space"),
            P("dp", None, "space"),
        ),
        check_vma=False,
    )
```

```python
import functools

import jax
import jax.numpy as jnp
from jax import lax
from jax.experimental import pallas as pl
from jax.experimental.pallas import tpu as pltpu
from jax.sharding import PartitionSpec as P

F32 = jnp.float32
BF16 = jnp.bfloat16
VMEM_LIMIT = 20 * 2**20
ROW_DOT = (((1,), (0,)), ((), ()))
LAST_DOT = (((1,), (1,)), ((), ()))
FIRST_DOT = (((0,), (0,)), ((), ()))


def dot(left, right, dims):
    return lax.dot_general(left, right, dims, preferred_element_type=F32)


def flat(value):
    return value.reshape(-1, value.shape[-1])


def shifted(value, step, cols):
    count = value.shape[0]
    moved = pltpu.roll(value, (-step) % count, 0)
    col = lax.broadcasted_iota(jnp.int32, value.shape, 0) % cols
    edge = cols - 1 if step == 1 else 0
    return jnp.where(col == edge, 0.0, moved)


def widened(parts, cols):
    return parts[1] + shifted(parts[0], -1, cols) + shifted(parts[2], 1, cols)


def narrowed(parts, cols):
    return parts[1] + shifted(parts[0], 1, cols) + shifted(parts[2], -1, cols)


def taps(sources, ws_ref, dims):
    sums = []
    for b in range(3):
        acc = None
        for a in range(3):
            part = dot(sources[a], ws_ref[a, b], dims)
            acc = part if acc is None else acc + part
        sums.append(acc)
    return sums


def edge_kernel(top_ref, end_ref, w_ref, first_ref, last_ref):
    for source, out in ((top_ref, first_ref), (end_ref, last_ref)):
        out[...] = jnp.maximum(dot(source[0], w_ref[...], ROW_DOT), 0.0).astype(BF16)


def inner_kernel(x_ref, wr_ref, first_ref, last_ref, ws_ref, we_ref, h_ref, h2_ref, s_ref):
    rows, cols, _ = h_ref.shape
    inside = rows - 2
    x_in = flat(x_ref[1 : rows - 1])
    h_in = jnp.maximum(dot(x_in, wr_ref[...], ROW_DOT), 0.0).astype(BF16)
    h_ref[0] = first_ref[...]
    h_ref[rows - 1] = last_ref[...]
    h_ref[1 : rows - 1] = h_in.reshape(inside, cols, -1)
    sums = taps([flat(h_ref[a : a + inside]) for a in range(3)], ws_ref, ROW_DOT)
    h_two = jnp.maximum(widened(sums, cols), 0.0).astype(BF16)
    h2_ref[...] = h_two
    pre = dot(h_two, we_ref[...], ROW_DOT) + x_in.astype(F32)
    s_ref[...] = jnp.maximum(pre, 0.0).astype(BF16).reshape(s_ref.shape)


def outer_kernel(
    h_ref, h2i_ref, above_ref, below_ref, ws_ref, we_ref, x_ref, si_ref, hp_ref, h2_ref, s_ref
):
    rows, cols, _ = h_ref.shape
    devices, split, channels = si_ref.shape
    inside = h2i_ref.shape[0]
    s_ref[:, :split] = si_ref[...]
    hp_ref[0] = above_ref[...]
    hp_ref[1 : rows + 1] = h_ref[...]
    hp_ref[rows + 1] = below_ref[...]
    tops = [above_ref[...], h_ref[0], h_ref[1]]
    ends = [h_ref[rows - 2], h_ref[rows - 1], below_ref[...]]
    sources = [jnp.concatenate(pair, axis=0) for pair in zip(tops, ends)]
    h_two = jnp.maximum(widened(taps(sources, ws_ref, ROW_DOT), cols), 0.0).astype(BF16)
    h2_ref[:inside] = h2i_ref[...]
    h2_ref[inside:] = h_two
    x_out = jnp.concatenate([x_ref[0], x_ref[rows - 1]], axis=0)
    pre = dot(h_two, we_ref[...], ROW_DOT) + x_out.astype(F32)
    s_ref[:, split:] = jnp.maximum(pre, 0.0).astype(BF16).reshape(devices, -1, channels)


def gram_kernel(parts_ref, s_ref, t_ref, out_ref):
    images, chunk, _ = s_ref.shape
    group = 16 if chunk % 16 == 0 else chunk
    count = images * group
    row = lax.broadcasted_iota(jnp.int32, (count, count), 0)
    col = lax.broadcasted_iota(jnp.int32, (count, count), 1)
    same = (row % group) == (col % group)
    image = lax.broadcasted_iota(jnp.int32, (images, count), 0)
    other = lax.broadcasted_iota(jnp.int32, (images, count), 1) // group
    slot_row = lax.broadcasted_iota(jnp.int32, (images, 128), 0)
    slot = lax.broadcasted_iota(jnp.int32, (images, 128), 1)
    message = jnp.zeros((images, 128), F32)
    for base, value_ref in ((0, s_ref), (3, t_ref)):
        gram = None
        for start in range(0, chunk, group):
            value = flat(value_ref[:, start : start + group])
            part = dot(value, value, LAST_DOT)
            gram = part if gram is None else gram + part
        gram = jnp.where(same, gram, 0.0).reshape(images, group, count).sum(axis=1)
        for k in range(3):
            partner = image if k == 0 else image ^ parts_ref[k - 1, 0]
            column = jnp.where(other == partner, gram, 0.0).sum(axis=1, keepdims=True)
            message = message + jnp.where(slot == 8 * slot_row + base + k, column, 0.0)
    out_ref[...] = jnp.broadcast_to(message.sum(axis=0, keepdims=True), out_ref.shape)


def grad_kernel(scale, parts_ref, msg_ref, s_ref, g_ref, loss_ref):
    images = s_ref.shape[0]
    total = jnp.broadcast_to(msg_ref[...].sum(axis=0, keepdims=True), (images, 128))
    row = lax.broadcasted_iota(jnp.int32, (images, 128), 0)
    lane = lax.broadcasted_iota(jnp.int32, (images, 128), 1)

    def column(k):
        return jnp.where(lane == 8 * row + k, total, 0.0).sum(axis=1, keepdims=True)

    v_s = [column(k) for k in range(3)]
    v_t = [column(3 + k) for k in range(3)]
    nu_s = jnp.sqrt(v_s[0] * v_s[0] + v_s[1] * v_s[1] + v_s[2] * v_s[2] + 1e-06)
    nu_t = jnp.sqrt(v_t[0] * v_t[0] + v_t[1] * v_t[1] + v_t[2] * v_t[2] + 1e-06)
    n_s = [v / nu_s for v in v_s]
    diff = [a - b / nu_t for a, b in zip(n_s, v_t)]
    terms = diff[0] * diff[0] + diff[1] * diff[1] + diff[2] * diff[2]
    loss_ref[...] = terms.sum(axis=0, keepdims=True)
    err = [2.0 * d for d in diff]
    inner = err[0] * n_s[0] + err[1] * n_s[1] + err[2] * n_s[2]
    coefs = [(e - inner * n) / nu_s for e, n in zip(err, n_s)]
    weights = [2.0 * coefs[0]]
    for k in range(2):
        own = coefs[k + 1]
        as_row = jnp.where(row == lane, own, 0.0).sum(axis=0, keepdims=True)
        partner = row ^ parts_ref[k, 0]
        theirs = jnp.where(lane == partner, as_row, 0.0).sum(axis=1, keepdims=True)
        weights.append(own + theirs)
    for i in range(images):
        own = s_ref[i].astype(F32)
        acc = weights[0][i : i + 1] * own
        for k in range(2):
            acc = acc + weights[k + 1][i : i + 1] * s_ref[i ^ parts_ref[k, 0]].astype(F32)
        g_ref[i] = jnp.where(own > 0.0, scale * acc, 0.0).astype(BF16)


def halves(g_ref, inside):
    split = inside // g_ref.shape[0]
    return flat(g_ref[:, :split]), flat(g_ref[:, split:])


def back_kernel(g_ref, h2_ref, we_ref, g2_ref, first_ref, last_ref):
    rows, cols, _ = g2_ref.shape
    inside = (rows - 2) * cols
    g_in, g_out = halves(g_ref, inside)
    back = dot(g_out, we_ref[...], LAST_DOT)
    g_two = jnp.where(h2_ref[inside:] > 0, back, 0.0).astype(BF16)
    first_ref[...] = g_two[:cols]
    last_ref[...] = g_two[cols:]
    g2_ref[0] = g_two[:cols]
    g2_ref[rows - 1] = g_two[cols:]
    back = dot(g_in, we_ref[...], LAST_DOT)
    g_two = jnp.where(h2_ref[:inside] > 0, back, 0.0).astype(BF16)
    g2_ref[1 : rows - 1] = g_two.reshape(rows - 2, cols, -1)


def farthest(place_ref, local_ref, up_ref, down_ref):
    depth = local_ref.shape[0] // 2
    block = 2 * ((place_ref[0] // 2 + depth // 2) % depth)
    up_ref[...] = local_ref[block]
    down_ref[...] = local_ref[block + 1]


def window_kernel(
    place_ref, g_ref, h2_ref, g2_ref, hp_ref, ws_ref, out_ref, g1_ref, up_ref, down_ref
):
    rows, cols, mid = g2_ref.shape
    chunks = out_ref.shape[0]
    width = mid // chunks
    inside = (rows - 2) * cols
    g_in, g_out = halves(g_ref, inside)
    expand = dot(g_in, h2_ref[:inside], FIRST_DOT) + dot(g_out, h2_ref[inside:], FIRST_DOT)
    part = expand.shape[0] // chunks
    out_ref[:, :part] = expand.astype(BF16).reshape(chunks, part, mid)
    g_two = flat(g2_ref[...])
    wide = g_two.astype(F32)
    moved = [shifted(wide, 1, cols).astype(BF16), g_two, shifted(wide, -1, cols).astype(BF16)]
    for a in range(3):
        source = flat(hp_ref[a : a + rows])
        for b in range(3):
            start = part + (3 * a + b) * width
            grad = dot(moved[b], source, FIRST_DOT).astype(BF16)
            out_ref[:, start : start + width] = grad.reshape(chunks, width, mid)
    farthest(place_ref, out_ref, up_ref, down_ref)
    sums = taps([flat(g2_ref[2 - a : rows - a]) for a in range(3)], ws_ref, LAST_DOT)
    total = narrowed(sums, cols)
    g1_ref[...] = jnp.where(flat(hp_ref[2:rows]) > 0, total, 0.0).astype(BF16)


def backward_kernel(
    place_ref, g2_ref, above_ref, below_ref, hp_ref, ws_ref, x_ref, g1i_ref,
    out_ref, g1o_ref, up_ref, down_ref,
):
    rows = g2_ref.shape[0]
    cols = g2_ref.shape[1]
    tops = [g2_ref[1], g2_ref[0], above_ref[...]]
    ends = [below_ref[...], g2_ref[rows - 1], g2_ref[rows - 2]]
    sources = [jnp.concatenate(pair, axis=0) for pair in zip(tops, ends)]
    total = narrowed(taps(sources, ws_ref, LAST_DOT), cols)
    h_out = jnp.concatenate([hp_ref[1], hp_ref[rows]], axis=0)
    g_one = jnp.where(h_out > 0, total, 0.0).astype(BF16)
    g1o_ref[...] = g_one
    x_out = jnp.concatenate([x_ref[0], x_ref[rows - 1]], axis=0)
    grad = dot(x_out, g_one, FIRST_DOT) + dot(flat(x_ref[1 : rows - 1]), g1i_ref[...], FIRST_DOT)
    out_ref[...] = grad.astype(BF16).reshape(out_ref.shape)
    farthest(place_ref, out_ref, up_ref, down_ref)


def images_kernel(g_ref, g1i_ref, g1o_ref, wr_ref, out_ref):
    _, rows, cols, _ = out_ref.shape
    g_in, g_out = halves(g_ref, g1i_ref.shape[0])
    inner = (g_in.astype(F32) + dot(g1i_ref[...], wr_ref[...], LAST_DOT)).astype(BF16)
    outer = (g_out.astype(F32) + dot(g1o_ref[...], wr_ref[...], LAST_DOT)).astype(BF16)
    out_ref[0, 0] = outer[:cols]
    out_ref[0, rows - 1] = outer[cols:]
    out_ref[0, 1 : rows - 1] = inner.reshape(rows - 2, cols, -1)


def add_kernel(offset, first, last, place_ref, early_ref, late_ref, *refs):
    rows = early_ref.shape[1]
    depth = early_ref.shape[0] // 2
    z, half = place_ref[0] // 2, place_ref[0] % 2
    outs = list(refs[4:] if first else refs[2:])
    if first:
        give_ref = outs.pop()
        block = 2 * z + 1 - half
        give_ref[:rows] = early_ref[block]
        give_ref[rows:] = late_ref[block]
    for way, sign in enumerate((1, -1)):
        block = 2 * ((z + sign * offset + depth) % depth)
        for index, side in enumerate((half, 1 - half) if last else (0, 1)):
            early = early_ref[block + side].astype(F32)
            late = late_ref[block + side].astype(F32)
            if first:
                here = jnp.where(side == way, 1.0, 0.0).astype(F32)
                early = early + here * refs[way][...].astype(F32)
                late = late + here * refs[2 + way][...].astype(F32)
            else:
                early = early + refs[way][side, :rows].astype(F32)
                late = late + refs[way][side, rows:].astype(F32)
            target = outs[2 * way + index] if last else outs[way].at[side]
            target[:rows] = early.astype(BF16)
            target[rows:] = late.astype(BF16)


def last_kernel(
    place_ref, early_ref, late_ref, own_ref, us, uc, ds, dc, expand_ref, spatial_ref, reduce_ref
):
    rows = early_ref.shape[1]
    block = place_ref[0]
    early = early_ref[block].astype(F32)
    late = late_ref[block].astype(F32)
    for ref in (own_ref, us, uc, ds, dc):
        early = early + ref[:rows].astype(F32)
        late = late + ref[rows:].astype(F32)
    part = expand_ref.shape[0]
    expand_ref[...] = early[:part]
    spatial_ref[...] = early[part:].reshape(spatial_ref.shape)
    reduce_ref[...] = late


def call(kernel, outs, flops, smem=0, scratch=()):
    def run(*args):
        specs = [
            pl.BlockSpec(memory_space=pltpu.SMEM if i < smem else pltpu.VMEM)
            for i in range(len(args))
        ]
        moved = sum(v.size * v.dtype.itemsize for v in args)
        return pl.pallas_call(
            kernel,
            out_shape=[jax.ShapeDtypeStruct(s, d) for s, d in outs],
            in_specs=specs,
            out_specs=[pl.BlockSpec(memory_space=pltpu.VMEM) for _ in outs],
            scratch_shapes=list(scratch),
            compiler_params=pltpu.CompilerParams(vmem_limit_bytes=VMEM_LIMIT),
            cost_estimate=pl.CostEstimate(flops=flops, bytes_accessed=moved, transcendentals=0),
        )(*args)

    return run


def exchanged(first, last):
    peers = lax.axis_size("space")
    up = [(i, i + 1) for i in range(peers - 1)]
    down = [(i + 1, i) for i in range(peers - 1)]
    return lax.ppermute(last, "space", up), lax.ppermute(first, "space", down)


def scattered(early, late, early_sends, late_sends, place):
    peers = lax.axis_size("space")
    far = peers // 4
    ups = [(i, (i + 2) % peers) for i in range(peers)]
    downs = [(i, (i - 2) % peers) for i in range(peers)]
    rows, mid = early.shape[1] + late.shape[1], early.shape[2]

    def moved(up, down):
        up = lax.ppermute(up, "space", ups)
        down = lax.ppermute(down, "space", downs)
        return up, down

    got = moved(*early_sends) + moved(*late_sends)
    for step in range(2, far + 1):
        first, last = step == 2, step == far
        kernel = functools.partial(add_kernel, far + 1 - step, first, last)
        half = ((rows, mid), BF16)
        outs = [half] * 4 if last else [((2, rows, mid), BF16)] * 2
        outs = outs + [half] * first
        got = list(call(kernel, outs, rows * mid, smem=1)(place, early, late, *got))
        if first:
            own = lax.ppermute(got.pop(), "space", [(i, i ^ 1) for i in range(peers)])
        if not last:
            got = moved(*got)
    cross_ups = [(i, j ^ 1) for i, j in ups]
    cross_downs = [(i, j ^ 1) for i, j in downs]
    sends = ((1, cross_ups), (3, cross_downs), (0, ups), (2, downs))
    ended = []
    for index, path in sends:
        ended.append(lax.ppermute(got[index], "space", path))
    return own, *ended


def step(images, teacher, w_reduce, w_spatial, w_expand, partners):
    _, rows, cols, channels = images.shape
    mid = w_reduce.shape[1]
    n_dp, n_space = lax.axis_size("dp"), lax.axis_size("space")
    pixels = rows * cols
    chunk = pixels // n_dp
    inside, outside = (rows - 2) * cols, 2 * cols
    split = inside // n_dp
    elems = float(pixels * n_space * channels)
    world = n_dp * n_space
    x = images.reshape(rows, cols, channels)
    place = lax.axis_index("space").reshape(1)
    teacher, place = lax.optimization_barrier((teacher, place))

    t_all = lax.all_to_all(teacher.reshape(n_dp, chunk, channels), "dp", 0, 0, tiled=True)
    first, last = pl.pallas_call(
        edge_kernel,
        grid=(1,),
        in_specs=[
            pl.BlockSpec((1, cols, channels), lambda i: (0, 0, 0)),
            pl.BlockSpec((1, cols, channels), lambda i: (rows - 1, 0, 0)),
            pl.BlockSpec((channels, mid), lambda i: (0, 0)),
        ],
        out_specs=[pl.BlockSpec((cols, mid), lambda i: (0, 0))] * 2,
        out_shape=[jax.ShapeDtypeStruct((cols, mid), BF16)] * 2,
        compiler_params=pltpu.CompilerParams(vmem_limit_bytes=VMEM_LIMIT),
        name="edge",
    )(x, x, w_reduce)
    above, below = exchanged(first, last)
    mac = 2 * cols * mid * mid
    h_one, h_in, s_in = call(
        inner_kernel,
        [
            ((rows, cols, mid), BF16),
            ((inside, mid), BF16),
            ((n_dp, split, channels), BF16),
        ],
        26 * mac,
    )(x, w_reduce, first, last, w_spatial, w_expand)
    h_pad, h_two, s_all = call(
        outer_kernel,
        [
            ((rows + 2, cols, mid), BF16),
            ((pixels, mid), BF16),
            ((n_dp, chunk, channels), BF16),
        ],
        26 * mac,
    )(h_one, h_in, above, below, w_spatial, w_expand, x, s_in)
    s_all = lax.all_to_all(s_all, "dp", 0, 0, tiled=True)

    (message,) = call(gram_kernel, [((world, 128), F32)], 32 * mac, smem=1)(partners, s_all, t_all)
    message = lax.all_to_all(message, ("dp", "space"), 0, 0, tiled=True)
    grads, loss = call(
        functools.partial(grad_kernel, elems),
        [((n_dp, chunk, channels), BF16), ((1, 1), F32)],
        mac,
        smem=1,
    )(partners, message, s_all)
    grads = lax.all_to_all(grads, "dp", 0, 0, tiled=True)
    g_two, first, last = call(
        back_kernel, [((rows, cols, mid), BF16), ((cols, mid), BF16), ((cols, mid), BF16)], 16 * mac
    )(grads, h_two, w_expand)
    over, under = exchanged(first, last)
    part, width = channels // n_space, mid // n_space
    early, g1_in, *early_sends = call(
        window_kernel,
        [((n_space, part + 9 * width, mid), BF16), ((inside, mid), BF16)]
        + [((part + 9 * width, mid), BF16)] * 2,
        70 * mac,
        smem=1,
    )(place, grads, h_two, g_two, h_pad, w_spatial)
    late, g1_out, *late_sends = call(
        backward_kernel,
        [((n_space, part, mid), BF16), ((outside, mid), BF16)] + [((part, mid), BF16)] * 2,
        34 * mac,
        smem=1,
    )(place, g_two, over, under, h_pad, w_spatial, x, g1_in)
    (g_images,) = call(
        images_kernel, [((1, rows, cols, channels), BF16)], 16 * mac
    )(grads, g1_in, g1_out, w_reduce)
    g_expand, g_spatial, g_reduce = call(
        last_kernel,
        [((part, mid), F32), ((3, 3, width, mid), F32), ((part, mid), F32)],
        mac,
        smem=1,
    )(place, early, late, *scattered(early, late, early_sends, late_sends, place))
    return (
        loss[0, 0],
        g_images,
        g_reduce[None],
        g_spatial.swapaxes(2, 3)[None],
        g_expand.T[None],
    )


def solution(mesh):
    return jax.shard_map(
        step,
        mesh=mesh,
        in_specs=(P("dp", "space", None, None), P("dp", "space", None, None), P(), P(), P(), P()),
        out_specs=(
            P(),
            P("dp", "space", None, None),
            P("dp", "space", None),
            P("dp", None, None, None, "space"),
            P("dp", None, "space"),
        ),
        check_vma=False,
    )
```

```python
import functools

import jax
import jax.numpy as jnp
from jax import lax
from jax.experimental import pallas as pl
from jax.experimental.pallas import tpu as pltpu
from jax.sharding import PartitionSpec as P

F32 = jnp.float32
BF16 = jnp.bfloat16
VMEM_LIMIT = 20 * 2**20
ROW_DOT = (((1,), (0,)), ((), ()))
LAST_DOT = (((1,), (1,)), ((), ()))
FIRST_DOT = (((0,), (0,)), ((), ()))


def dot(left, right, dims):
    return lax.dot_general(left, right, dims, preferred_element_type=F32)


def flat(value):
    return value.reshape(-1, value.shape[-1])


def shifted(value, step, cols):
    count = value.shape[0]
    moved = pltpu.roll(value, (-step) % count, 0)
    col = lax.broadcasted_iota(jnp.int32, value.shape, 0) % cols
    edge = cols - 1 if step == 1 else 0
    return jnp.where(col == edge, 0.0, moved)


def widened(parts, cols):
    return parts[1] + shifted(parts[0], -1, cols) + shifted(parts[2], 1, cols)


def narrowed(parts, cols):
    return parts[1] + shifted(parts[0], 1, cols) + shifted(parts[2], -1, cols)


def taps(sources, ws_ref, dims):
    sums = []
    for b in range(3):
        acc = None
        for a in range(3):
            part = dot(sources[a], ws_ref[a, b], dims)
            acc = part if acc is None else acc + part
        sums.append(acc)
    return sums


def edge_kernel(top_ref, end_ref, w_ref, first_ref, last_ref):
    for source, out in ((top_ref, first_ref), (end_ref, last_ref)):
        out[...] = jnp.maximum(dot(source[0], w_ref[...], ROW_DOT), 0.0).astype(BF16)


def inner_kernel(x_ref, wr_ref, first_ref, last_ref, ws_ref, we_ref, h_ref, h2_ref, s_ref):
    rows, cols, _ = h_ref.shape
    inside = rows - 2
    x_in = flat(x_ref[1 : rows - 1])
    h_in = jnp.maximum(dot(x_in, wr_ref[...], ROW_DOT), 0.0).astype(BF16)
    h_ref[0] = first_ref[...]
    h_ref[rows - 1] = last_ref[...]
    h_ref[1 : rows - 1] = h_in.reshape(inside, cols, -1)
    sums = taps([flat(h_ref[a : a + inside]) for a in range(3)], ws_ref, ROW_DOT)
    h_two = jnp.maximum(widened(sums, cols), 0.0).astype(BF16)
    h2_ref[...] = h_two
    pre = dot(h_two, we_ref[...], ROW_DOT) + x_in.astype(F32)
    s_ref[...] = jnp.maximum(pre, 0.0).astype(BF16).reshape(s_ref.shape)


def outer_kernel(
    h_ref, h2i_ref, above_ref, below_ref, ws_ref, we_ref, x_ref, si_ref, hp_ref, h2_ref, s_ref
):
    rows, cols, _ = h_ref.shape
    devices, split, channels = si_ref.shape
    inside = h2i_ref.shape[0]
    s_ref[:, :split] = si_ref[...]
    hp_ref[0] = above_ref[...]
    hp_ref[1 : rows + 1] = h_ref[...]
    hp_ref[rows + 1] = below_ref[...]
    tops = [above_ref[...], h_ref[0], h_ref[1]]
    ends = [h_ref[rows - 2], h_ref[rows - 1], below_ref[...]]
    sources = [jnp.concatenate(pair, axis=0) for pair in zip(tops, ends)]
    h_two = jnp.maximum(widened(taps(sources, ws_ref, ROW_DOT), cols), 0.0).astype(BF16)
    h2_ref[:inside] = h2i_ref[...]
    h2_ref[inside:] = h_two
    x_out = jnp.concatenate([x_ref[0], x_ref[rows - 1]], axis=0)
    pre = dot(h_two, we_ref[...], ROW_DOT) + x_out.astype(F32)
    s_ref[:, split:] = jnp.maximum(pre, 0.0).astype(BF16).reshape(devices, -1, channels)


def gram_kernel(parts_ref, s_ref, t_ref, out_ref):
    images, chunk, _ = s_ref.shape
    group = 16 if chunk % 16 == 0 else chunk
    count = images * group
    row = lax.broadcasted_iota(jnp.int32, (count, count), 0)
    col = lax.broadcasted_iota(jnp.int32, (count, count), 1)
    same = (row % group) == (col % group)
    image = lax.broadcasted_iota(jnp.int32, (images, count), 0)
    other = lax.broadcasted_iota(jnp.int32, (images, count), 1) // group
    slot_row = lax.broadcasted_iota(jnp.int32, (images, 128), 0)
    slot = lax.broadcasted_iota(jnp.int32, (images, 128), 1)
    message = jnp.zeros((images, 128), F32)
    for base, value_ref in ((0, s_ref), (3, t_ref)):
        gram = None
        for start in range(0, chunk, group):
            value = flat(value_ref[:, start : start + group])
            part = dot(value, value, LAST_DOT)
            gram = part if gram is None else gram + part
        gram = jnp.where(same, gram, 0.0).reshape(images, group, count).sum(axis=1)
        for k in range(3):
            partner = image if k == 0 else image ^ parts_ref[k - 1, 0]
            column = jnp.where(other == partner, gram, 0.0).sum(axis=1, keepdims=True)
            message = message + jnp.where(slot == 8 * slot_row + base + k, column, 0.0)
    out_ref[...] = jnp.broadcast_to(message.sum(axis=0, keepdims=True), out_ref.shape)


def grad_kernel(scale, parts_ref, msg_ref, s_ref, g_ref, loss_ref):
    images = s_ref.shape[0]
    total = jnp.broadcast_to(msg_ref[...].sum(axis=0, keepdims=True), (images, 128))
    row = lax.broadcasted_iota(jnp.int32, (images, 128), 0)
    lane = lax.broadcasted_iota(jnp.int32, (images, 128), 1)

    def column(k):
        return jnp.where(lane == 8 * row + k, total, 0.0).sum(axis=1, keepdims=True)

    v_s = [column(k) for k in range(3)]
    v_t = [column(3 + k) for k in range(3)]
    nu_s = jnp.sqrt(v_s[0] * v_s[0] + v_s[1] * v_s[1] + v_s[2] * v_s[2] + 1e-06)
    nu_t = jnp.sqrt(v_t[0] * v_t[0] + v_t[1] * v_t[1] + v_t[2] * v_t[2] + 1e-06)
    n_s = [v / nu_s for v in v_s]
    diff = [a - b / nu_t for a, b in zip(n_s, v_t)]
    terms = diff[0] * diff[0] + diff[1] * diff[1] + diff[2] * diff[2]
    loss_ref[...] = terms.sum(axis=0, keepdims=True)
    err = [2.0 * d for d in diff]
    inner = err[0] * n_s[0] + err[1] * n_s[1] + err[2] * n_s[2]
    coefs = [(e - inner * n) / nu_s for e, n in zip(err, n_s)]
    weights = [2.0 * coefs[0]]
    for k in range(2):
        own = coefs[k + 1]
        as_row = jnp.where(row == lane, own, 0.0).sum(axis=0, keepdims=True)
        partner = row ^ parts_ref[k, 0]
        theirs = jnp.where(lane == partner, as_row, 0.0).sum(axis=1, keepdims=True)
        weights.append(own + theirs)
    for i in range(images):
        own = s_ref[i].astype(F32)
        acc = weights[0][i : i + 1] * own
        for k in range(2):
            acc = acc + weights[k + 1][i : i + 1] * s_ref[i ^ parts_ref[k, 0]].astype(F32)
        g_ref[i] = jnp.where(own > 0.0, scale * acc, 0.0).astype(BF16)


def halves(g_ref, inside):
    split = inside // g_ref.shape[0]
    return flat(g_ref[:, :split]), flat(g_ref[:, split:])


def back_kernel(g_ref, h2_ref, we_ref, g2_ref, first_ref, last_ref):
    rows, cols, _ = g2_ref.shape
    inside = (rows - 2) * cols
    g_in, g_out = halves(g_ref, inside)
    back = dot(g_out, we_ref[...], LAST_DOT)
    g_two = jnp.where(h2_ref[inside:] > 0, back, 0.0).astype(BF16)
    first_ref[...] = g_two[:cols]
    last_ref[...] = g_two[cols:]
    g2_ref[0] = g_two[:cols]
    g2_ref[rows - 1] = g_two[cols:]
    back = dot(g_in, we_ref[...], LAST_DOT)
    g_two = jnp.where(h2_ref[:inside] > 0, back, 0.0).astype(BF16)
    g2_ref[1 : rows - 1] = g_two.reshape(rows - 2, cols, -1)


def farthest(place_ref, local_ref, up_ref, down_ref):
    depth = local_ref.shape[0] // 2
    block = 2 * ((place_ref[0] // 2 + depth // 2) % depth)
    up_ref[...] = local_ref[block]
    down_ref[...] = local_ref[block + 1]


def window_kernel(
    place_ref, g_ref, h2_ref, g2_ref, hp_ref, ws_ref,
    out_ref, g1_ref, up_ref, down_ref, near_ref,
):
    rows, cols, mid = g2_ref.shape
    chunks = out_ref.shape[0]
    width = mid // chunks
    inside = (rows - 2) * cols
    g_in, g_out = halves(g_ref, inside)
    expand = dot(g_in, h2_ref[:inside], FIRST_DOT) + dot(g_out, h2_ref[inside:], FIRST_DOT)
    part = expand.shape[0] // chunks
    out_ref[:, :part] = expand.astype(BF16).reshape(chunks, part, mid)
    g_two = flat(g2_ref[...])
    wide = g_two.astype(F32)
    moved = [shifted(wide, 1, cols).astype(BF16), g_two, shifted(wide, -1, cols).astype(BF16)]
    for a in range(3):
        source = flat(hp_ref[a : a + rows])
        for b in range(3):
            start = part + (3 * a + b) * width
            grad = dot(moved[b], source, FIRST_DOT).astype(BF16)
            out_ref[:, start : start + width] = grad.reshape(chunks, width, mid)
    farthest(place_ref, out_ref, up_ref, down_ref)
    near_others(place_ref, out_ref, near_ref)
    sums = taps([flat(g2_ref[2 - a : rows - a]) for a in range(3)], ws_ref, LAST_DOT)
    total = narrowed(sums, cols)
    g1_ref[...] = jnp.where(flat(hp_ref[2:rows]) > 0, total, 0.0).astype(BF16)


def backward_kernel(
    place_ref, g2_ref, above_ref, below_ref, hp_ref, ws_ref, x_ref, g1i_ref,
    out_ref, g1o_ref, up_ref, down_ref,
):
    rows = g2_ref.shape[0]
    cols = g2_ref.shape[1]
    tops = [g2_ref[1], g2_ref[0], above_ref[...]]
    ends = [below_ref[...], g2_ref[rows - 1], g2_ref[rows - 2]]
    sources = [jnp.concatenate(pair, axis=0) for pair in zip(tops, ends)]
    total = narrowed(taps(sources, ws_ref, LAST_DOT), cols)
    h_out = jnp.concatenate([hp_ref[1], hp_ref[rows]], axis=0)
    g_one = jnp.where(h_out > 0, total, 0.0).astype(BF16)
    g1o_ref[...] = g_one
    x_out = jnp.concatenate([x_ref[0], x_ref[rows - 1]], axis=0)
    grad = dot(x_out, g_one, FIRST_DOT) + dot(flat(x_ref[1 : rows - 1]), g1i_ref[...], FIRST_DOT)
    out_ref[...] = grad.astype(BF16).reshape(out_ref.shape)
    farthest(place_ref, out_ref, up_ref, down_ref)


def images_kernel(g_ref, g1i_ref, g1o_ref, wr_ref, out_ref):
    _, rows, cols, _ = out_ref.shape
    g_in, g_out = halves(g_ref, g1i_ref.shape[0])
    inner = (g_in.astype(F32) + dot(g1i_ref[...], wr_ref[...], LAST_DOT)).astype(BF16)
    outer = (g_out.astype(F32) + dot(g1o_ref[...], wr_ref[...], LAST_DOT)).astype(BF16)
    out_ref[0, 0] = outer[:cols]
    out_ref[0, rows - 1] = outer[cols:]
    out_ref[0, 1 : rows - 1] = inner.reshape(rows - 2, cols, -1)


def near_others(place_ref, local_ref, out_ref):
    depth = local_ref.shape[0] // 2
    z, half = place_ref[0] // 2, place_ref[0] % 2
    for index in range(3):
        out_ref[index] = local_ref[2 * ((z + index - 1 + depth) % depth) + 1 - half]


def join_kernel(
    offset, place_ref, early_ref, late_ref, eu, ed, lu, ld, up_ref, down_ref, near_ref
):
    rows = early_ref.shape[1]
    depth = early_ref.shape[0] // 2
    near_others(place_ref, late_ref, near_ref)
    for way, (sign, got, out_ref) in enumerate(((1, (eu, lu), up_ref), (-1, (ed, ld), down_ref))):
        block = 2 * ((place_ref[0] // 2 + sign * offset + depth) % depth)
        for side in range(2):
            early, late = early_ref[block + side], late_ref[block + side]
            if side == way:
                early = (early.astype(F32) + got[0][...].astype(F32)).astype(BF16)
                late = (late.astype(F32) + got[1][...].astype(F32)).astype(BF16)
            out_ref[side, :rows] = early
            out_ref[side, rows:] = late


def pass_kernel(offset, split, place_ref, early_ref, late_ref, gu_ref, gd_ref, *outs):
    rows = early_ref.shape[1]
    depth = early_ref.shape[0] // 2
    z, half = place_ref[0] // 2, place_ref[0] % 2
    for way, (sign, got_ref) in enumerate(((1, gu_ref), (-1, gd_ref))):
        block = 2 * ((z + sign * offset + depth) % depth)
        for index, side in enumerate((half, 1 - half) if split else (0, 1)):
            early = early_ref[block + side].astype(F32) + got_ref[side, :rows].astype(F32)
            late = late_ref[block + side].astype(F32) + got_ref[side, rows:].astype(F32)
            target = outs[2 * way + index] if split else outs[way].at[side]
            target[:rows] = early.astype(BF16)
            target[rows:] = late.astype(BF16)


def own_terms(place_ref, early_ref, late_ref, ne_ref, nl_ref, offset):
    depth = early_ref.shape[0] // 2
    z, half = place_ref[0] // 2, place_ref[0] % 2
    block = 2 * ((z + offset + depth) % depth) + half
    early = early_ref[block].astype(F32) + ne_ref[1 + offset].astype(F32)
    return early, late_ref[block].astype(F32) + nl_ref[1 + offset].astype(F32)


def side_kernel(
    place_ref, early_ref, late_ref, ne_ref, nl_ref, us, uc, ds, dc, up_ref, down_ref
):
    rows = early_ref.shape[1]
    for offset, got, out_ref in ((1, (us, uc), up_ref), (-1, (ds, dc), down_ref)):
        early, late = own_terms(place_ref, early_ref, late_ref, ne_ref, nl_ref, offset)
        for ref in got:
            early = early + ref[:rows].astype(F32)
            late = late + ref[rows:].astype(F32)
        out_ref[:rows] = early.astype(BF16)
        out_ref[rows:] = late.astype(BF16)


def last_kernel(
    place_ref, early_ref, late_ref, ne_ref, nl_ref, gu_ref, gd_ref,
    expand_ref, spatial_ref, reduce_ref,
):
    rows = early_ref.shape[1]
    early, late = own_terms(place_ref, early_ref, late_ref, ne_ref, nl_ref, 0)
    for ref in (gu_ref, gd_ref):
        early = early + ref[:rows].astype(F32)
        late = late + ref[rows:].astype(F32)
    part = expand_ref.shape[0]
    expand_ref[...] = early[:part]
    spatial_ref[...] = early[part:].reshape(spatial_ref.shape)
    reduce_ref[...] = late


def call(kernel, outs, flops, smem=0, scratch=()):
    def run(*args):
        specs = [
            pl.BlockSpec(memory_space=pltpu.SMEM if i < smem else pltpu.VMEM)
            for i in range(len(args))
        ]
        moved = sum(v.size * v.dtype.itemsize for v in args)
        return pl.pallas_call(
            kernel,
            out_shape=[jax.ShapeDtypeStruct(s, d) for s, d in outs],
            in_specs=specs,
            out_specs=[pl.BlockSpec(memory_space=pltpu.VMEM) for _ in outs],
            scratch_shapes=list(scratch),
            compiler_params=pltpu.CompilerParams(vmem_limit_bytes=VMEM_LIMIT),
            cost_estimate=pl.CostEstimate(flops=flops, bytes_accessed=moved, transcendentals=0),
        )(*args)

    return run


def exchanged(first, last):
    peers = lax.axis_size("space")
    up = [(i, i + 1) for i in range(peers - 1)]
    down = [(i + 1, i) for i in range(peers - 1)]
    return lax.ppermute(last, "space", up), lax.ppermute(first, "space", down)


def scattered(early, late, early_sends, late_sends, near_early, place):
    peers = lax.axis_size("space")
    far = peers // 4
    ups = [(i, (i + 2) % peers) for i in range(peers)]
    downs = [(i, (i - 2) % peers) for i in range(peers)]
    swap = [(i, i ^ 1) for i in range(peers)]
    rows, mid = early.shape[1] + late.shape[1], early.shape[2]
    side = ((rows, mid), BF16)
    pair = [((2, rows, mid), BF16)] * 2

    def sent(value, path):
        return lax.ppermute(value, "space", path)

    def moved(up, down):
        return sent(up, ups), sent(down, downs)

    got = moved(*early_sends)
    near_early = sent(near_early, swap)
    got = got + moved(*late_sends)
    near = ((3, *late.shape[1:]), BF16)
    join = functools.partial(join_kernel, far - 1)
    up, down, near_late = call(join, pair + [near], rows * mid, smem=1)(place, early, late, *got)
    up, down = moved(up, down)
    near_late = sent(near_late, swap)
    for step in range(3, far):
        split = step == far - 1
        kernel = functools.partial(pass_kernel, far + 1 - step, split)
        outs = [side] * 4 if split else pair
        got = call(kernel, outs, rows * mid, smem=1)(place, early, late, up, down)
        if not split:
            up, down = moved(*got)
    uc = sent(got[1], [(i, j ^ 1) for i, j in ups])
    dc = sent(got[3], [(i, j ^ 1) for i, j in downs])
    us, ds = moved(got[0], got[2])
    terms = (place, early, late, near_early, near_late)
    up, down = call(side_kernel, [side] * 2, rows * mid, smem=1)(*terms, us, uc, ds, dc)
    return *terms, *moved(up, down)


def step(images, teacher, w_reduce, w_spatial, w_expand, partners):
    _, rows, cols, channels = images.shape
    mid = w_reduce.shape[1]
    n_dp, n_space = lax.axis_size("dp"), lax.axis_size("space")
    pixels = rows * cols
    chunk = pixels // n_dp
    inside, outside = (rows - 2) * cols, 2 * cols
    split = inside // n_dp
    elems = float(pixels * n_space * channels)
    world = n_dp * n_space
    x = images.reshape(rows, cols, channels)
    place = lax.axis_index("space").reshape(1)
    teacher, place = lax.optimization_barrier((teacher, place))

    t_all = lax.all_to_all(teacher.reshape(n_dp, chunk, channels), "dp", 0, 0, tiled=True)
    first, last = pl.pallas_call(
        edge_kernel,
        grid=(1,),
        in_specs=[
            pl.BlockSpec((1, cols, channels), lambda i: (0, 0, 0)),
            pl.BlockSpec((1, cols, channels), lambda i: (rows - 1, 0, 0)),
            pl.BlockSpec((channels, mid), lambda i: (0, 0)),
        ],
        out_specs=[pl.BlockSpec((cols, mid), lambda i: (0, 0))] * 2,
        out_shape=[jax.ShapeDtypeStruct((cols, mid), BF16)] * 2,
        compiler_params=pltpu.CompilerParams(vmem_limit_bytes=VMEM_LIMIT),
        name="edge",
    )(x, x, w_reduce)
    above, below = exchanged(first, last)
    mac = 2 * cols * mid * mid
    h_one, h_in, s_in = call(
        inner_kernel,
        [
            ((rows, cols, mid), BF16),
            ((inside, mid), BF16),
            ((n_dp, split, channels), BF16),
        ],
        26 * mac,
    )(x, w_reduce, first, last, w_spatial, w_expand)
    h_pad, h_two, s_all = call(
        outer_kernel,
        [
            ((rows + 2, cols, mid), BF16),
            ((pixels, mid), BF16),
            ((n_dp, chunk, channels), BF16),
        ],
        26 * mac,
    )(h_one, h_in, above, below, w_spatial, w_expand, x, s_in)
    s_all = lax.all_to_all(s_all, "dp", 0, 0, tiled=True)

    (message,) = call(gram_kernel, [((world, 128), F32)], 32 * mac, smem=1)(partners, s_all, t_all)
    message = lax.all_to_all(message, ("dp", "space"), 0, 0, tiled=True)
    grads, loss = call(
        functools.partial(grad_kernel, elems),
        [((n_dp, chunk, channels), BF16), ((1, 1), F32)],
        mac,
        smem=1,
    )(partners, message, s_all)
    grads = lax.all_to_all(grads, "dp", 0, 0, tiled=True)
    g_two, first, last = call(
        back_kernel, [((rows, cols, mid), BF16), ((cols, mid), BF16), ((cols, mid), BF16)], 16 * mac
    )(grads, h_two, w_expand)
    over, under = exchanged(first, last)
    part, width = channels // n_space, mid // n_space
    early, g1_in, *early_sends, near_early = call(
        window_kernel,
        [((n_space, part + 9 * width, mid), BF16), ((inside, mid), BF16)]
        + [((part + 9 * width, mid), BF16)] * 2
        + [((3, part + 9 * width, mid), BF16)],
        70 * mac,
        smem=1,
    )(place, grads, h_two, g_two, h_pad, w_spatial)
    late, g1_out, *late_sends = call(
        backward_kernel,
        [((n_space, part, mid), BF16), ((outside, mid), BF16)] + [((part, mid), BF16)] * 2,
        34 * mac,
        smem=1,
    )(place, g_two, over, under, h_pad, w_spatial, x, g1_in)
    (g_images,) = call(
        images_kernel, [((1, rows, cols, channels), BF16)], 16 * mac
    )(grads, g1_in, g1_out, w_reduce)
    g_expand, g_spatial, g_reduce = call(
        last_kernel,
        [((part, mid), F32), ((3, 3, width, mid), F32), ((part, mid), F32)],
        mac,
        smem=1,
    )(*scattered(early, late, early_sends, late_sends, near_early, place))
    return (
        loss[0, 0],
        g_images,
        g_reduce[None],
        g_spatial.swapaxes(2, 3)[None],
        g_expand.T[None],
    )


def solution(mesh):
    return jax.shard_map(
        step,
        mesh=mesh,
        in_specs=(P("dp", "space", None, None), P("dp", "space", None, None), P(), P(), P(), P()),
        out_specs=(
            P(),
            P("dp", "space", None, None),
            P("dp", "space", None),
            P("dp", None, None, None, "space"),
            P("dp", None, "space"),
        ),
        check_vma=False,
    )
```

```python
import functools

import jax
import jax.numpy as jnp
from jax import lax
from jax.experimental import pallas as pl
from jax.experimental.pallas import tpu as pltpu
from jax.sharding import PartitionSpec as P

F32 = jnp.float32
BF16 = jnp.bfloat16
VMEM_LIMIT = 20 * 2**20
ROW_DOT = (((1,), (0,)), ((), ()))
LAST_DOT = (((1,), (1,)), ((), ()))
FIRST_DOT = (((0,), (0,)), ((), ()))


def dot(left, right, dims):
    return lax.dot_general(left, right, dims, preferred_element_type=F32)


def flat(value):
    return value.reshape(-1, value.shape[-1])


def shifted(value, step, cols):
    count = value.shape[0]
    moved = pltpu.roll(value, (-step) % count, 0)
    col = lax.broadcasted_iota(jnp.int32, value.shape, 0) % cols
    edge = cols - 1 if step == 1 else 0
    return jnp.where(col == edge, 0.0, moved)


def widened(parts, cols):
    return parts[1] + shifted(parts[0], -1, cols) + shifted(parts[2], 1, cols)


def narrowed(parts, cols):
    return parts[1] + shifted(parts[0], 1, cols) + shifted(parts[2], -1, cols)


def taps(sources, ws_ref, dims):
    sums = []
    for b in range(3):
        acc = None
        for a in range(3):
            part = dot(sources[a], ws_ref[a, b], dims)
            acc = part if acc is None else acc + part
        sums.append(acc)
    return sums


def edge_kernel(top_ref, end_ref, w_ref, first_ref, last_ref):
    for source, out in ((top_ref, first_ref), (end_ref, last_ref)):
        out[...] = jnp.maximum(dot(source[0], w_ref[...], ROW_DOT), 0.0).astype(BF16)


def inner_kernel(x_ref, wr_ref, first_ref, last_ref, ws_ref, we_ref, h_ref, h2_ref, s_ref):
    rows, cols, _ = h_ref.shape
    inside = rows - 2
    x_in = flat(x_ref[1 : rows - 1])
    h_in = jnp.maximum(dot(x_in, wr_ref[...], ROW_DOT), 0.0).astype(BF16)
    h_ref[0] = first_ref[...]
    h_ref[rows - 1] = last_ref[...]
    h_ref[1 : rows - 1] = h_in.reshape(inside, cols, -1)
    sums = taps([flat(h_ref[a : a + inside]) for a in range(3)], ws_ref, ROW_DOT)
    h_two = jnp.maximum(widened(sums, cols), 0.0).astype(BF16)
    h2_ref[...] = h_two
    pre = dot(h_two, we_ref[...], ROW_DOT) + x_in.astype(F32)
    s_ref[...] = jnp.maximum(pre, 0.0).astype(BF16).reshape(s_ref.shape)


def outer_kernel(
    h_ref, h2i_ref, above_ref, below_ref, ws_ref, we_ref, x_ref, si_ref, hp_ref, h2_ref, s_ref
):
    rows, cols, _ = h_ref.shape
    devices, split, channels = si_ref.shape
    inside = h2i_ref.shape[0]
    s_ref[:, :split] = si_ref[...]
    hp_ref[0] = above_ref[...]
    hp_ref[1 : rows + 1] = h_ref[...]
    hp_ref[rows + 1] = below_ref[...]
    tops = [above_ref[...], h_ref[0], h_ref[1]]
    ends = [h_ref[rows - 2], h_ref[rows - 1], below_ref[...]]
    sources = [jnp.concatenate(pair, axis=0) for pair in zip(tops, ends)]
    h_two = jnp.maximum(widened(taps(sources, ws_ref, ROW_DOT), cols), 0.0).astype(BF16)
    h2_ref[:inside] = h2i_ref[...]
    h2_ref[inside:] = h_two
    x_out = jnp.concatenate([x_ref[0], x_ref[rows - 1]], axis=0)
    pre = dot(h_two, we_ref[...], ROW_DOT) + x_out.astype(F32)
    s_ref[:, split:] = jnp.maximum(pre, 0.0).astype(BF16).reshape(devices, -1, channels)


def gram_kernel(parts_ref, s_ref, t_ref, out_ref):
    images, chunk, _ = s_ref.shape
    group = 16 if chunk % 16 == 0 else chunk
    count = images * group
    row = lax.broadcasted_iota(jnp.int32, (count, count), 0)
    col = lax.broadcasted_iota(jnp.int32, (count, count), 1)
    same = (row % group) == (col % group)
    image = lax.broadcasted_iota(jnp.int32, (images, count), 0)
    other = lax.broadcasted_iota(jnp.int32, (images, count), 1) // group
    slot_row = lax.broadcasted_iota(jnp.int32, (images, 128), 0)
    slot = lax.broadcasted_iota(jnp.int32, (images, 128), 1)
    message = jnp.zeros((images, 128), F32)
    for base, value_ref in ((0, s_ref), (3, t_ref)):
        gram = None
        for start in range(0, chunk, group):
            value = flat(value_ref[:, start : start + group])
            part = dot(value, value, LAST_DOT)
            gram = part if gram is None else gram + part
        gram = jnp.where(same, gram, 0.0).reshape(images, group, count).sum(axis=1)
        for k in range(3):
            partner = image if k == 0 else image ^ parts_ref[k - 1, 0]
            column = jnp.where(other == partner, gram, 0.0).sum(axis=1, keepdims=True)
            message = message + jnp.where(slot == 8 * slot_row + base + k, column, 0.0)
    out_ref[...] = jnp.broadcast_to(message.sum(axis=0, keepdims=True), out_ref.shape)


def grad_kernel(scale, parts_ref, msg_ref, s_ref, g_ref, loss_ref):
    images = s_ref.shape[0]
    total = jnp.broadcast_to(msg_ref[...].sum(axis=0, keepdims=True), (images, 128))
    row = lax.broadcasted_iota(jnp.int32, (images, 128), 0)
    lane = lax.broadcasted_iota(jnp.int32, (images, 128), 1)

    def column(k):
        return jnp.where(lane == 8 * row + k, total, 0.0).sum(axis=1, keepdims=True)

    v_s = [column(k) for k in range(3)]
    v_t = [column(3 + k) for k in range(3)]
    nu_s = jnp.sqrt(v_s[0] * v_s[0] + v_s[1] * v_s[1] + v_s[2] * v_s[2] + 1e-06)
    nu_t = jnp.sqrt(v_t[0] * v_t[0] + v_t[1] * v_t[1] + v_t[2] * v_t[2] + 1e-06)
    n_s = [v / nu_s for v in v_s]
    diff = [a - b / nu_t for a, b in zip(n_s, v_t)]
    terms = diff[0] * diff[0] + diff[1] * diff[1] + diff[2] * diff[2]
    loss_ref[...] = terms.sum(axis=0, keepdims=True)
    err = [2.0 * d for d in diff]
    inner = err[0] * n_s[0] + err[1] * n_s[1] + err[2] * n_s[2]
    coefs = [(e - inner * n) / nu_s for e, n in zip(err, n_s)]
    weights = [2.0 * coefs[0]]
    for k in range(2):
        own = coefs[k + 1]
        as_row = jnp.where(row == lane, own, 0.0).sum(axis=0, keepdims=True)
        partner = row ^ parts_ref[k, 0]
        theirs = jnp.where(lane == partner, as_row, 0.0).sum(axis=1, keepdims=True)
        weights.append(own + theirs)
    for i in range(images):
        own = s_ref[i].astype(F32)
        acc = weights[0][i : i + 1] * own
        for k in range(2):
            acc = acc + weights[k + 1][i : i + 1] * s_ref[i ^ parts_ref[k, 0]].astype(F32)
        g_ref[i] = jnp.where(own > 0.0, scale * acc, 0.0).astype(BF16)


def halves(g_ref, inside):
    split = inside // g_ref.shape[0]
    return flat(g_ref[:, :split]), flat(g_ref[:, split:])


def back_kernel(g_ref, h2_ref, we_ref, g2_ref, first_ref, last_ref):
    rows, cols, _ = g2_ref.shape
    inside = (rows - 2) * cols
    g_in, g_out = halves(g_ref, inside)
    back = dot(g_out, we_ref[...], LAST_DOT)
    g_two = jnp.where(h2_ref[inside:] > 0, back, 0.0).astype(BF16)
    first_ref[...] = g_two[:cols]
    last_ref[...] = g_two[cols:]
    g2_ref[0] = g_two[:cols]
    g2_ref[rows - 1] = g_two[cols:]
    back = dot(g_in, we_ref[...], LAST_DOT)
    g_two = jnp.where(h2_ref[:inside] > 0, back, 0.0).astype(BF16)
    g2_ref[1 : rows - 1] = g_two.reshape(rows - 2, cols, -1)


def farthest(place_ref, local_ref, up_ref, down_ref):
    depth = local_ref.shape[0] // 2
    block = 2 * ((place_ref[0] // 2 + depth // 2) % depth)
    up_ref[...] = local_ref[block]
    down_ref[...] = local_ref[block + 1]


def window_kernel(
    place_ref, g_ref, h2_ref, g2_ref, hp_ref, ws_ref,
    out_ref, g1_ref, up_ref, down_ref,
):
    rows, cols, mid = g2_ref.shape
    chunks = out_ref.shape[0]
    width = mid // chunks
    inside = (rows - 2) * cols
    g_in, g_out = halves(g_ref, inside)
    expand = dot(g_in, h2_ref[:inside], FIRST_DOT) + dot(g_out, h2_ref[inside:], FIRST_DOT)
    part = expand.shape[0] // chunks
    out_ref[:, :part] = expand.astype(BF16).reshape(chunks, part, mid)
    g_two = flat(g2_ref[...])
    wide = g_two.astype(F32)
    moved = [shifted(wide, 1, cols).astype(BF16), g_two, shifted(wide, -1, cols).astype(BF16)]
    for a in range(3):
        source = flat(hp_ref[a : a + rows])
        for b in range(3):
            start = part + (3 * a + b) * width
            grad = dot(moved[b], source, FIRST_DOT).astype(BF16)
            out_ref[:, start : start + width] = grad.reshape(chunks, width, mid)
    farthest(place_ref, out_ref, up_ref, down_ref)
    sums = taps([flat(g2_ref[2 - a : rows - a]) for a in range(3)], ws_ref, LAST_DOT)
    total = narrowed(sums, cols)
    g1_ref[...] = jnp.where(flat(hp_ref[2:rows]) > 0, total, 0.0).astype(BF16)


def backward_kernel(
    place_ref, g2_ref, above_ref, below_ref, hp_ref, ws_ref, x_ref, g1i_ref,
    out_ref, g1o_ref, up_ref, down_ref,
):
    rows = g2_ref.shape[0]
    cols = g2_ref.shape[1]
    tops = [g2_ref[1], g2_ref[0], above_ref[...]]
    ends = [below_ref[...], g2_ref[rows - 1], g2_ref[rows - 2]]
    sources = [jnp.concatenate(pair, axis=0) for pair in zip(tops, ends)]
    total = narrowed(taps(sources, ws_ref, LAST_DOT), cols)
    h_out = jnp.concatenate([hp_ref[1], hp_ref[rows]], axis=0)
    g_one = jnp.where(h_out > 0, total, 0.0).astype(BF16)
    g1o_ref[...] = g_one
    x_out = jnp.concatenate([x_ref[0], x_ref[rows - 1]], axis=0)
    grad = dot(x_out, g_one, FIRST_DOT) + dot(flat(x_ref[1 : rows - 1]), g1i_ref[...], FIRST_DOT)
    out_ref[...] = grad.astype(BF16).reshape(out_ref.shape)
    farthest(place_ref, out_ref, up_ref, down_ref)


def images_kernel(g_ref, g1i_ref, g1o_ref, wr_ref, out_ref):
    _, rows, cols, _ = out_ref.shape
    g_in, g_out = halves(g_ref, g1i_ref.shape[0])
    inner = (g_in.astype(F32) + dot(g1i_ref[...], wr_ref[...], LAST_DOT)).astype(BF16)
    outer = (g_out.astype(F32) + dot(g1o_ref[...], wr_ref[...], LAST_DOT)).astype(BF16)
    out_ref[0, 0] = outer[:cols]
    out_ref[0, rows - 1] = outer[cols:]
    out_ref[0, 1 : rows - 1] = inner.reshape(rows - 2, cols, -1)


def near_others(place_ref, early_ref, late_ref, out_ref):
    rows = early_ref.shape[1]
    depth = early_ref.shape[0] // 2
    z, half = place_ref[0] // 2, place_ref[0] % 2
    for index in range(3):
        block = 2 * ((z + index - 1 + depth) % depth) + 1 - half
        out_ref[index, :rows] = early_ref[block]
        out_ref[index, rows:] = late_ref[block]


def join_kernel(
    offset, place_ref, early_ref, late_ref, eu, ed, lu, ld, up_ref, down_ref, near_ref
):
    rows = early_ref.shape[1]
    depth = early_ref.shape[0] // 2
    near_others(place_ref, early_ref, late_ref, near_ref)
    for way, (sign, got, out_ref) in enumerate(((1, (eu, lu), up_ref), (-1, (ed, ld), down_ref))):
        block = 2 * ((place_ref[0] // 2 + sign * offset + depth) % depth)
        for side in range(2):
            early, late = early_ref[block + side], late_ref[block + side]
            if side == way:
                early = (early.astype(F32) + got[0][...].astype(F32)).astype(BF16)
                late = (late.astype(F32) + got[1][...].astype(F32)).astype(BF16)
            out_ref[side, :rows] = early
            out_ref[side, rows:] = late


def pass_kernel(offset, split, place_ref, early_ref, late_ref, gu_ref, gd_ref, *outs):
    rows = early_ref.shape[1]
    depth = early_ref.shape[0] // 2
    z, half = place_ref[0] // 2, place_ref[0] % 2
    for way, (sign, got_ref) in enumerate(((1, gu_ref), (-1, gd_ref))):
        block = 2 * ((z + sign * offset + depth) % depth)
        for index, side in enumerate((half, 1 - half) if split else (0, 1)):
            early = early_ref[block + side].astype(F32) + got_ref[side, :rows].astype(F32)
            late = late_ref[block + side].astype(F32) + got_ref[side, rows:].astype(F32)
            target = outs[2 * way + index] if split else outs[way].at[side]
            target[:rows] = early.astype(BF16)
            target[rows:] = late.astype(BF16)


def own_terms(place_ref, early_ref, late_ref, near_ref, offset):
    rows = early_ref.shape[1]
    depth = early_ref.shape[0] // 2
    z, half = place_ref[0] // 2, place_ref[0] % 2
    block = 2 * ((z + offset + depth) % depth) + half
    early = early_ref[block].astype(F32) + near_ref[1 + offset, :rows].astype(F32)
    return early, late_ref[block].astype(F32) + near_ref[1 + offset, rows:].astype(F32)


def side_kernel(
    place_ref, early_ref, late_ref, near_ref, us, uc, ds, dc, up_ref, down_ref
):
    rows = early_ref.shape[1]
    for offset, got, out_ref in ((1, (us, uc), up_ref), (-1, (ds, dc), down_ref)):
        early, late = own_terms(place_ref, early_ref, late_ref, near_ref, offset)
        for ref in got:
            early = early + ref[:rows].astype(F32)
            late = late + ref[rows:].astype(F32)
        out_ref[:rows] = early.astype(BF16)
        out_ref[rows:] = late.astype(BF16)


def last_kernel(
    place_ref, early_ref, late_ref, near_ref, gu_ref, gd_ref,
    expand_ref, spatial_ref, reduce_ref,
):
    rows = early_ref.shape[1]
    early, late = own_terms(place_ref, early_ref, late_ref, near_ref, 0)
    for ref in (gu_ref, gd_ref):
        early = early + ref[:rows].astype(F32)
        late = late + ref[rows:].astype(F32)
    part = expand_ref.shape[0]
    expand_ref[...] = early[:part]
    spatial_ref[...] = early[part:].reshape(spatial_ref.shape)
    reduce_ref[...] = late


def call(kernel, outs, flops, smem=0, scratch=()):
    def run(*args):
        specs = [
            pl.BlockSpec(memory_space=pltpu.SMEM if i < smem else pltpu.VMEM)
            for i in range(len(args))
        ]
        moved = sum(v.size * v.dtype.itemsize for v in args)
        return pl.pallas_call(
            kernel,
            out_shape=[jax.ShapeDtypeStruct(s, d) for s, d in outs],
            in_specs=specs,
            out_specs=[pl.BlockSpec(memory_space=pltpu.VMEM) for _ in outs],
            scratch_shapes=list(scratch),
            compiler_params=pltpu.CompilerParams(vmem_limit_bytes=VMEM_LIMIT),
            cost_estimate=pl.CostEstimate(flops=flops, bytes_accessed=moved, transcendentals=0),
        )(*args)

    return run


def exchanged(first, last):
    peers = lax.axis_size("space")
    up = [(i, i + 1) for i in range(peers - 1)]
    down = [(i + 1, i) for i in range(peers - 1)]
    return lax.ppermute(last, "space", up), lax.ppermute(first, "space", down)


def scattered(early, late, early_sends, late_sends, place):
    peers = lax.axis_size("space")
    far = peers // 4
    ups = [(i, (i + 2) % peers) for i in range(peers)]
    downs = [(i, (i - 2) % peers) for i in range(peers)]
    swap = [(i, i ^ 1) for i in range(peers)]
    rows, mid = early.shape[1] + late.shape[1], early.shape[2]
    side = ((rows, mid), BF16)
    pair = [((2, rows, mid), BF16)] * 2

    def sent(value, path):
        return lax.ppermute(value, "space", path)

    def moved(up, down):
        return sent(up, ups), sent(down, downs)

    got = moved(*early_sends) + moved(*late_sends)
    near = ((3, rows, mid), BF16)
    join = functools.partial(join_kernel, far - 1)
    up, down, near = call(join, pair + [near], rows * mid, smem=1)(
        place, early, late, *got
    )
    up, down = moved(up, down)
    near = sent(near, swap)
    for step in range(3, far):
        split = step == far - 1
        kernel = functools.partial(pass_kernel, far + 1 - step, split)
        outs = [side] * 4 if split else pair
        got = call(kernel, outs, rows * mid, smem=1)(place, early, late, up, down)
        if not split:
            up, down = moved(*got)
    uc = sent(got[1], [(i, j ^ 1) for i, j in ups])
    dc = sent(got[3], [(i, j ^ 1) for i, j in downs])
    us, ds = moved(got[0], got[2])
    terms = (place, early, late, near)
    up, down = call(side_kernel, [side] * 2, rows * mid, smem=1)(*terms, us, uc, ds, dc)
    return *terms, *moved(up, down)


def step(images, teacher, w_reduce, w_spatial, w_expand, partners):
    _, rows, cols, channels = images.shape
    mid = w_reduce.shape[1]
    n_dp, n_space = lax.axis_size("dp"), lax.axis_size("space")
    pixels = rows * cols
    chunk = pixels // n_dp
    inside, outside = (rows - 2) * cols, 2 * cols
    split = inside // n_dp
    elems = float(pixels * n_space * channels)
    world = n_dp * n_space
    x = images.reshape(rows, cols, channels)
    place = lax.axis_index("space").reshape(1)
    teacher, place = lax.optimization_barrier((teacher, place))

    t_all = lax.all_to_all(teacher.reshape(n_dp, chunk, channels), "dp", 0, 0, tiled=True)
    first, last = pl.pallas_call(
        edge_kernel,
        grid=(1,),
        in_specs=[
            pl.BlockSpec((1, cols, channels), lambda i: (0, 0, 0)),
            pl.BlockSpec((1, cols, channels), lambda i: (rows - 1, 0, 0)),
            pl.BlockSpec((channels, mid), lambda i: (0, 0)),
        ],
        out_specs=[pl.BlockSpec((cols, mid), lambda i: (0, 0))] * 2,
        out_shape=[jax.ShapeDtypeStruct((cols, mid), BF16)] * 2,
        compiler_params=pltpu.CompilerParams(vmem_limit_bytes=VMEM_LIMIT),
        name="edge",
    )(x, x, w_reduce)
    above, below = exchanged(first, last)
    mac = 2 * cols * mid * mid
    h_one, h_in, s_in = call(
        inner_kernel,
        [
            ((rows, cols, mid), BF16),
            ((inside, mid), BF16),
            ((n_dp, split, channels), BF16),
        ],
        26 * mac,
    )(x, w_reduce, first, last, w_spatial, w_expand)
    h_pad, h_two, s_all = call(
        outer_kernel,
        [
            ((rows + 2, cols, mid), BF16),
            ((pixels, mid), BF16),
            ((n_dp, chunk, channels), BF16),
        ],
        26 * mac,
    )(h_one, h_in, above, below, w_spatial, w_expand, x, s_in)
    s_all = lax.all_to_all(s_all, "dp", 0, 0, tiled=True)

    (message,) = call(gram_kernel, [((world, 128), F32)], 32 * mac, smem=1)(partners, s_all, t_all)
    message = lax.all_to_all(message, ("dp", "space"), 0, 0, tiled=True)
    grads, loss = call(
        functools.partial(grad_kernel, elems),
        [((n_dp, chunk, channels), BF16), ((1, 1), F32)],
        mac,
        smem=1,
    )(partners, message, s_all)
    grads = lax.all_to_all(grads, "dp", 0, 0, tiled=True)
    g_two, first, last = call(
        back_kernel, [((rows, cols, mid), BF16), ((cols, mid), BF16), ((cols, mid), BF16)], 16 * mac
    )(grads, h_two, w_expand)
    over, under = exchanged(first, last)
    part, width = channels // n_space, mid // n_space
    early, g1_in, *early_sends = call(
        window_kernel,
        [((n_space, part + 9 * width, mid), BF16), ((inside, mid), BF16)]
        + [((part + 9 * width, mid), BF16)] * 2,
        70 * mac,
        smem=1,
    )(place, grads, h_two, g_two, h_pad, w_spatial)
    late, g1_out, *late_sends = call(
        backward_kernel,
        [((n_space, part, mid), BF16), ((outside, mid), BF16)] + [((part, mid), BF16)] * 2,
        34 * mac,
        smem=1,
    )(place, g_two, over, under, h_pad, w_spatial, x, g1_in)
    (g_images,) = call(
        images_kernel, [((1, rows, cols, channels), BF16)], 16 * mac
    )(grads, g1_in, g1_out, w_reduce)
    g_expand, g_spatial, g_reduce = call(
        last_kernel,
        [((part, mid), F32), ((3, 3, width, mid), F32), ((part, mid), F32)],
        mac,
        smem=1,
    )(*scattered(early, late, early_sends, late_sends, place))
    return (
        loss[0, 0],
        g_images,
        g_reduce[None],
        g_spatial.swapaxes(2, 3)[None],
        g_expand.T[None],
    )


def solution(mesh):
    return jax.shard_map(
        step,
        mesh=mesh,
        in_specs=(P("dp", "space", None, None), P("dp", "space", None, None), P(), P(), P(), P()),
        out_specs=(
            P(),
            P("dp", "space", None, None),
            P("dp", "space", None),
            P("dp", None, None, None, "space"),
            P("dp", None, "space"),
        ),
        check_vma=False,
    )
```

```python
import functools

import jax
import jax.numpy as jnp
from jax import lax
from jax.experimental import pallas as pl
from jax.experimental.pallas import tpu as pltpu
from jax.sharding import PartitionSpec as P

F32 = jnp.float32
BF16 = jnp.bfloat16
VMEM_LIMIT = 20 * 2**20
ROW_DOT = (((1,), (0,)), ((), ()))
LAST_DOT = (((1,), (1,)), ((), ()))
FIRST_DOT = (((0,), (0,)), ((), ()))


def dot(left, right, dims):
    return lax.dot_general(left, right, dims, preferred_element_type=F32)


def flat(value):
    return value.reshape(-1, value.shape[-1])


def shifted(value, step, cols):
    count = value.shape[0]
    moved = pltpu.roll(value, (-step) % count, 0)
    col = lax.broadcasted_iota(jnp.int32, value.shape, 0) % cols
    edge = cols - 1 if step == 1 else 0
    return jnp.where(col == edge, 0.0, moved)


def widened(parts, cols):
    return parts[1] + shifted(parts[0], -1, cols) + shifted(parts[2], 1, cols)


def narrowed(parts, cols):
    return parts[1] + shifted(parts[0], 1, cols) + shifted(parts[2], -1, cols)


def taps(sources, ws_ref, dims):
    sums = []
    for b in range(3):
        acc = None
        for a in range(3):
            part = dot(sources[a], ws_ref[a, b], dims)
            acc = part if acc is None else acc + part
        sums.append(acc)
    return sums


def edge_kernel(top_ref, end_ref, w_ref, first_ref, last_ref):
    for source, out in ((top_ref, first_ref), (end_ref, last_ref)):
        out[...] = jnp.maximum(dot(source[0], w_ref[...], ROW_DOT), 0.0).astype(BF16)


def inner_kernel(x_ref, wr_ref, first_ref, last_ref, ws_ref, we_ref, h_ref, h2_ref, s_ref):
    rows, cols, _ = h_ref.shape
    inside = rows - 2
    x_in = flat(x_ref[1 : rows - 1])
    h_in = jnp.maximum(dot(x_in, wr_ref[...], ROW_DOT), 0.0).astype(BF16)
    h_ref[0] = first_ref[...]
    h_ref[rows - 1] = last_ref[...]
    h_ref[1 : rows - 1] = h_in.reshape(inside, cols, -1)
    sums = taps([flat(h_ref[a : a + inside]) for a in range(3)], ws_ref, ROW_DOT)
    h_two = jnp.maximum(widened(sums, cols), 0.0).astype(BF16)
    h2_ref[...] = h_two
    pre = dot(h_two, we_ref[...], ROW_DOT) + x_in.astype(F32)
    s_ref[...] = jnp.maximum(pre, 0.0).astype(BF16).reshape(s_ref.shape)


def outer_kernel(
    h_ref, h2i_ref, above_ref, below_ref, ws_ref, we_ref, x_ref, si_ref, hp_ref, h2_ref, s_ref
):
    rows, cols, _ = h_ref.shape
    devices, split, channels = si_ref.shape
    inside = h2i_ref.shape[0]
    s_ref[:, :split] = si_ref[...]
    hp_ref[0] = above_ref[...]
    hp_ref[1 : rows + 1] = h_ref[...]
    hp_ref[rows + 1] = below_ref[...]
    tops = [above_ref[...], h_ref[0], h_ref[1]]
    ends = [h_ref[rows - 2], h_ref[rows - 1], below_ref[...]]
    sources = [jnp.concatenate(pair, axis=0) for pair in zip(tops, ends)]
    h_two = jnp.maximum(widened(taps(sources, ws_ref, ROW_DOT), cols), 0.0).astype(BF16)
    h2_ref[:inside] = h2i_ref[...]
    h2_ref[inside:] = h_two
    x_out = jnp.concatenate([x_ref[0], x_ref[rows - 1]], axis=0)
    pre = dot(h_two, we_ref[...], ROW_DOT) + x_out.astype(F32)
    s_ref[:, split:] = jnp.maximum(pre, 0.0).astype(BF16).reshape(devices, -1, channels)


def gram_kernel(parts_ref, s_ref, t_ref, out_ref):
    images, chunk, _ = s_ref.shape
    group = 16 if chunk % 16 == 0 else chunk
    count = images * group
    row = lax.broadcasted_iota(jnp.int32, (count, count), 0)
    col = lax.broadcasted_iota(jnp.int32, (count, count), 1)
    same = (row % group) == (col % group)
    image = lax.broadcasted_iota(jnp.int32, (images, count), 0)
    other = lax.broadcasted_iota(jnp.int32, (images, count), 1) // group
    slot_row = lax.broadcasted_iota(jnp.int32, (images, 128), 0)
    slot = lax.broadcasted_iota(jnp.int32, (images, 128), 1)
    message = jnp.zeros((images, 128), F32)
    for base, value_ref in ((0, s_ref), (3, t_ref)):
        gram = None
        for start in range(0, chunk, group):
            value = flat(value_ref[:, start : start + group])
            part = dot(value, value, LAST_DOT)
            gram = part if gram is None else gram + part
        gram = jnp.where(same, gram, 0.0).reshape(images, group, count).sum(axis=1)
        for k in range(3):
            partner = image if k == 0 else image ^ parts_ref[k - 1, 0]
            column = jnp.where(other == partner, gram, 0.0).sum(axis=1, keepdims=True)
            message = message + jnp.where(slot == 8 * slot_row + base + k, column, 0.0)
    out_ref[...] = jnp.broadcast_to(message.sum(axis=0, keepdims=True), out_ref.shape)


def grad_kernel(scale, parts_ref, msg_ref, s_ref, g_ref, loss_ref):
    images = s_ref.shape[0]
    total = jnp.broadcast_to(msg_ref[...].sum(axis=0, keepdims=True), (images, 128))
    row = lax.broadcasted_iota(jnp.int32, (images, 128), 0)
    lane = lax.broadcasted_iota(jnp.int32, (images, 128), 1)

    def column(k):
        return jnp.where(lane == 8 * row + k, total, 0.0).sum(axis=1, keepdims=True)

    v_s = [column(k) for k in range(3)]
    v_t = [column(3 + k) for k in range(3)]
    nu_s = jnp.sqrt(v_s[0] * v_s[0] + v_s[1] * v_s[1] + v_s[2] * v_s[2] + 1e-06)
    nu_t = jnp.sqrt(v_t[0] * v_t[0] + v_t[1] * v_t[1] + v_t[2] * v_t[2] + 1e-06)
    n_s = [v / nu_s for v in v_s]
    diff = [a - b / nu_t for a, b in zip(n_s, v_t)]
    terms = diff[0] * diff[0] + diff[1] * diff[1] + diff[2] * diff[2]
    loss_ref[...] = terms.sum(axis=0, keepdims=True)
    err = [2.0 * d for d in diff]
    inner = err[0] * n_s[0] + err[1] * n_s[1] + err[2] * n_s[2]
    coefs = [(e - inner * n) / nu_s for e, n in zip(err, n_s)]
    weights = [2.0 * coefs[0]]
    for k in range(2):
        own = coefs[k + 1]
        as_row = jnp.where(row == lane, own, 0.0).sum(axis=0, keepdims=True)
        partner = row ^ parts_ref[k, 0]
        theirs = jnp.where(lane == partner, as_row, 0.0).sum(axis=1, keepdims=True)
        weights.append(own + theirs)
    for i in range(images):
        own = s_ref[i].astype(F32)
        acc = weights[0][i : i + 1] * own
        for k in range(2):
            acc = acc + weights[k + 1][i : i + 1] * s_ref[i ^ parts_ref[k, 0]].astype(F32)
        g_ref[i] = jnp.where(own > 0.0, scale * acc, 0.0).astype(BF16)


def halves(g_ref, inside):
    split = inside // g_ref.shape[0]
    return flat(g_ref[:, :split]), flat(g_ref[:, split:])


def back_kernel(g_ref, h2_ref, we_ref, g2_ref, first_ref, last_ref):
    rows, cols, _ = g2_ref.shape
    inside = (rows - 2) * cols
    g_in, g_out = halves(g_ref, inside)
    back = dot(g_out, we_ref[...], LAST_DOT)
    g_two = jnp.where(h2_ref[inside:] > 0, back, 0.0).astype(BF16)
    first_ref[...] = g_two[:cols]
    last_ref[...] = g_two[cols:]
    g2_ref[0] = g_two[:cols]
    g2_ref[rows - 1] = g_two[cols:]
    back = dot(g_in, we_ref[...], LAST_DOT)
    g_two = jnp.where(h2_ref[:inside] > 0, back, 0.0).astype(BF16)
    g2_ref[1 : rows - 1] = g_two.reshape(rows - 2, cols, -1)


def farthest(place_ref, local_ref, up_ref, down_ref):
    depth = local_ref.shape[0] // 2
    block = 2 * ((place_ref[0] // 2 + depth // 2) % depth)
    up_ref[...] = local_ref[block]
    down_ref[...] = local_ref[block + 1]


def window_kernel(
    place_ref, g_ref, h2_ref, g2_ref, hp_ref, ws_ref,
    out_ref, g1_ref, up_ref, down_ref,
):
    rows, cols, mid = g2_ref.shape
    chunks = out_ref.shape[0]
    width = mid // chunks
    inside = (rows - 2) * cols
    g_in, g_out = halves(g_ref, inside)
    expand = dot(g_in, h2_ref[:inside], FIRST_DOT) + dot(g_out, h2_ref[inside:], FIRST_DOT)
    part = expand.shape[0] // chunks
    out_ref[:, :part] = expand.astype(BF16).reshape(chunks, part, mid)
    g_two = flat(g2_ref[...])
    wide = g_two.astype(F32)
    moved = [shifted(wide, 1, cols).astype(BF16), g_two, shifted(wide, -1, cols).astype(BF16)]
    for a in range(3):
        source = flat(hp_ref[a : a + rows])
        for b in range(3):
            start = part + (3 * a + b) * width
            grad = dot(moved[b], source, FIRST_DOT).astype(BF16)
            out_ref[:, start : start + width] = grad.reshape(chunks, width, mid)
    farthest(place_ref, out_ref, up_ref, down_ref)
    sums = taps([flat(g2_ref[2 - a : rows - a]) for a in range(3)], ws_ref, LAST_DOT)
    total = narrowed(sums, cols)
    g1_ref[...] = jnp.where(flat(hp_ref[2:rows]) > 0, total, 0.0).astype(BF16)


def backward_kernel(
    place_ref, g2_ref, above_ref, below_ref, hp_ref, ws_ref, x_ref, g1i_ref,
    out_ref, g1o_ref, up_ref, down_ref,
):
    rows = g2_ref.shape[0]
    cols = g2_ref.shape[1]
    tops = [g2_ref[1], g2_ref[0], above_ref[...]]
    ends = [below_ref[...], g2_ref[rows - 1], g2_ref[rows - 2]]
    sources = [jnp.concatenate(pair, axis=0) for pair in zip(tops, ends)]
    total = narrowed(taps(sources, ws_ref, LAST_DOT), cols)
    h_out = jnp.concatenate([hp_ref[1], hp_ref[rows]], axis=0)
    g_one = jnp.where(h_out > 0, total, 0.0).astype(BF16)
    g1o_ref[...] = g_one
    x_out = jnp.concatenate([x_ref[0], x_ref[rows - 1]], axis=0)
    grad = dot(x_out, g_one, FIRST_DOT) + dot(flat(x_ref[1 : rows - 1]), g1i_ref[...], FIRST_DOT)
    out_ref[...] = grad.astype(BF16).reshape(out_ref.shape)
    farthest(place_ref, out_ref, up_ref, down_ref)


def images_kernel(g_ref, g1i_ref, g1o_ref, wr_ref, out_ref):
    _, rows, cols, _ = out_ref.shape
    g_in, g_out = halves(g_ref, g1i_ref.shape[0])
    inner = (g_in.astype(F32) + dot(g1i_ref[...], wr_ref[...], LAST_DOT)).astype(BF16)
    outer = (g_out.astype(F32) + dot(g1o_ref[...], wr_ref[...], LAST_DOT)).astype(BF16)
    out_ref[0, 0] = outer[:cols]
    out_ref[0, rows - 1] = outer[cols:]
    out_ref[0, 1 : rows - 1] = inner.reshape(rows - 2, cols, -1)


def near_others(place_ref, early_ref, late_ref, out_ref):
    rows = early_ref.shape[1]
    depth = early_ref.shape[0] // 2
    z, half = place_ref[0] // 2, place_ref[0] % 2
    for index in range(3):
        block = 2 * ((z + index - 1 + depth) % depth) + 1 - half
        out_ref[index, :rows] = early_ref[block]
        out_ref[index, rows:] = late_ref[block]


def join_kernel(offset, place_ref, local_ref, gu_ref, gd_ref, up_ref, down_ref):
    depth = local_ref.shape[0] // 2
    for way, (sign, got_ref, out_ref) in enumerate(((1, gu_ref, up_ref), (-1, gd_ref, down_ref))):
        block = 2 * ((place_ref[0] // 2 + sign * offset + depth) % depth)
        out_ref[1 - way] = local_ref[block + 1 - way]
        total = local_ref[block + way].astype(F32) + got_ref[...].astype(F32)
        out_ref[way] = total.astype(BF16)


def late_kernel(
    offset, place_ref, early_ref, late_ref, gu_ref, gd_ref, up_ref, down_ref, near_ref
):
    join_kernel(offset, place_ref, late_ref, gu_ref, gd_ref, up_ref, down_ref)
    near_others(place_ref, early_ref, late_ref, near_ref)


def cross_kernel(
    offset, place_ref, early_ref, late_ref, eu_ref, ed_ref, lu_ref, ld_ref, us, uc, ds, dc
):
    rows = early_ref.shape[1]
    depth = early_ref.shape[0] // 2
    z, half = place_ref[0] // 2, place_ref[0] % 2
    for sign, e_ref, l_ref, outs in ((1, eu_ref, lu_ref, (us, uc)), (-1, ed_ref, ld_ref, (ds, dc))):
        block = 2 * ((z + sign * offset + depth) % depth)
        for side, target in zip((half, 1 - half), outs):
            early = early_ref[block + side].astype(F32) + e_ref[side].astype(F32)
            late = late_ref[block + side].astype(F32) + l_ref[side].astype(F32)
            target[:rows] = early.astype(BF16)
            target[rows:] = late.astype(BF16)


def own_terms(place_ref, early_ref, late_ref, near_ref, offset):
    rows = early_ref.shape[1]
    depth = early_ref.shape[0] // 2
    z, half = place_ref[0] // 2, place_ref[0] % 2
    block = 2 * ((z + offset + depth) % depth) + half
    early = early_ref[block].astype(F32) + near_ref[1 + offset, :rows].astype(F32)
    return early, late_ref[block].astype(F32) + near_ref[1 + offset, rows:].astype(F32)


def side_kernel(
    place_ref, early_ref, late_ref, near_ref, us, uc, ds, dc, up_ref, down_ref
):
    rows = early_ref.shape[1]
    for offset, got, out_ref in ((1, (us, uc), up_ref), (-1, (ds, dc), down_ref)):
        early, late = own_terms(place_ref, early_ref, late_ref, near_ref, offset)
        for ref in got:
            early = early + ref[:rows].astype(F32)
            late = late + ref[rows:].astype(F32)
        out_ref[:rows] = early.astype(BF16)
        out_ref[rows:] = late.astype(BF16)


def last_kernel(
    place_ref, early_ref, late_ref, near_ref, gu_ref, gd_ref,
    expand_ref, spatial_ref, reduce_ref,
):
    rows = early_ref.shape[1]
    early, late = own_terms(place_ref, early_ref, late_ref, near_ref, 0)
    for ref in (gu_ref, gd_ref):
        early = early + ref[:rows].astype(F32)
        late = late + ref[rows:].astype(F32)
    part = expand_ref.shape[0]
    expand_ref[...] = early[:part]
    spatial_ref[...] = early[part:].reshape(spatial_ref.shape)
    reduce_ref[...] = late


def call(kernel, outs, flops, smem=0, scratch=()):
    def run(*args):
        specs = [
            pl.BlockSpec(memory_space=pltpu.SMEM if i < smem else pltpu.VMEM)
            for i in range(len(args))
        ]
        moved = sum(v.size * v.dtype.itemsize for v in args)
        return pl.pallas_call(
            kernel,
            out_shape=[jax.ShapeDtypeStruct(s, d) for s, d in outs],
            in_specs=specs,
            out_specs=[pl.BlockSpec(memory_space=pltpu.VMEM) for _ in outs],
            scratch_shapes=list(scratch),
            compiler_params=pltpu.CompilerParams(vmem_limit_bytes=VMEM_LIMIT),
            cost_estimate=pl.CostEstimate(flops=flops, bytes_accessed=moved, transcendentals=0),
        )(*args)

    return run


def exchanged(first, last):
    peers = lax.axis_size("space")
    up = [(i, i + 1) for i in range(peers - 1)]
    down = [(i + 1, i) for i in range(peers - 1)]
    return lax.ppermute(last, "space", up), lax.ppermute(first, "space", down)


def scattered(early, late, early_sends, late_sends, place):
    peers = lax.axis_size("space")
    far = peers // 4
    ups = [(i, (i + 2) % peers) for i in range(peers)]
    downs = [(i, (i - 2) % peers) for i in range(peers)]
    swap = [(i, i ^ 1) for i in range(peers)]
    rows, mid = early.shape[1] + late.shape[1], early.shape[2]
    side = ((rows, mid), BF16)
    near = ((3, rows, mid), BF16)
    pairs = [[((2, *local.shape[1:]), BF16)] * 2 for local in (early, late)]
    assert far == 4

    def sent(value, path):
        return lax.ppermute(value, "space", path)

    def moved(up, down):
        return sent(up, ups), sent(down, downs)

    early_got = moved(*early_sends)
    late_got = moved(*late_sends)
    join = functools.partial(join_kernel, far - 1)
    early_got = call(join, pairs[0], rows * mid, smem=1)(place, early, *early_got)
    early_got = moved(*early_got)
    join = functools.partial(late_kernel, far - 1)
    *late_got, near = call(join, pairs[1] + [near], rows * mid, smem=1)(
        place, early, late, *late_got
    )
    late_got = moved(*late_got)
    near = sent(near, swap)
    cross = functools.partial(cross_kernel, far - 2)
    got = call(cross, [side] * 4, rows * mid, smem=1)(place, early, late, *early_got, *late_got)
    uc = sent(got[1], [(i, j ^ 1) for i, j in ups])
    dc = sent(got[3], [(i, j ^ 1) for i, j in downs])
    us, ds = moved(got[0], got[2])
    terms = (place, early, late, near)
    up, down = call(side_kernel, [side] * 2, rows * mid, smem=1)(*terms, us, uc, ds, dc)
    return *terms, *moved(up, down)


def step(images, teacher, w_reduce, w_spatial, w_expand, partners):
    _, rows, cols, channels = images.shape
    mid = w_reduce.shape[1]
    n_dp, n_space = lax.axis_size("dp"), lax.axis_size("space")
    pixels = rows * cols
    chunk = pixels // n_dp
    inside, outside = (rows - 2) * cols, 2 * cols
    split = inside // n_dp
    elems = float(pixels * n_space * channels)
    world = n_dp * n_space
    x = images.reshape(rows, cols, channels)
    place = lax.axis_index("space").reshape(1)
    teacher, place = lax.optimization_barrier((teacher, place))

    t_all = lax.all_to_all(teacher.reshape(n_dp, chunk, channels), "dp", 0, 0, tiled=True)
    first, last = pl.pallas_call(
        edge_kernel,
        grid=(1,),
        in_specs=[
            pl.BlockSpec((1, cols, channels), lambda i: (0, 0, 0)),
            pl.BlockSpec((1, cols, channels), lambda i: (rows - 1, 0, 0)),
            pl.BlockSpec((channels, mid), lambda i: (0, 0)),
        ],
        out_specs=[pl.BlockSpec((cols, mid), lambda i: (0, 0))] * 2,
        out_shape=[jax.ShapeDtypeStruct((cols, mid), BF16)] * 2,
        compiler_params=pltpu.CompilerParams(vmem_limit_bytes=VMEM_LIMIT),
        name="edge",
    )(x, x, w_reduce)
    above, below = exchanged(first, last)
    mac = 2 * cols * mid * mid
    h_one, h_in, s_in = call(
        inner_kernel,
        [
            ((rows, cols, mid), BF16),
            ((inside, mid), BF16),
            ((n_dp, split, channels), BF16),
        ],
        26 * mac,
    )(x, w_reduce, first, last, w_spatial, w_expand)
    h_pad, h_two, s_all = call(
        outer_kernel,
        [
            ((rows + 2, cols, mid), BF16),
            ((pixels, mid), BF16),
            ((n_dp, chunk, channels), BF16),
        ],
        26 * mac,
    )(h_one, h_in, above, below, w_spatial, w_expand, x, s_in)
    s_all = lax.all_to_all(s_all, "dp", 0, 0, tiled=True)

    (message,) = call(gram_kernel, [((world, 128), F32)], 32 * mac, smem=1)(partners, s_all, t_all)
    message = lax.all_to_all(message, ("dp", "space"), 0, 0, tiled=True)
    grads, loss = call(
        functools.partial(grad_kernel, elems),
        [((n_dp, chunk, channels), BF16), ((1, 1), F32)],
        mac,
        smem=1,
    )(partners, message, s_all)
    grads = lax.all_to_all(grads, "dp", 0, 0, tiled=True)
    g_two, first, last = call(
        back_kernel, [((rows, cols, mid), BF16), ((cols, mid), BF16), ((cols, mid), BF16)], 16 * mac
    )(grads, h_two, w_expand)
    over, under = exchanged(first, last)
    part, width = channels // n_space, mid // n_space
    early, g1_in, *early_sends = call(
        window_kernel,
        [((n_space, part + 9 * width, mid), BF16), ((inside, mid), BF16)]
        + [((part + 9 * width, mid), BF16)] * 2,
        70 * mac,
        smem=1,
    )(place, grads, h_two, g_two, h_pad, w_spatial)
    late, g1_out, *late_sends = call(
        backward_kernel,
        [((n_space, part, mid), BF16), ((outside, mid), BF16)] + [((part, mid), BF16)] * 2,
        34 * mac,
        smem=1,
    )(place, g_two, over, under, h_pad, w_spatial, x, g1_in)
    (g_images,) = call(
        images_kernel, [((1, rows, cols, channels), BF16)], 16 * mac
    )(grads, g1_in, g1_out, w_reduce)
    g_expand, g_spatial, g_reduce = call(
        last_kernel,
        [((part, mid), F32), ((3, 3, width, mid), F32), ((part, mid), F32)],
        mac,
        smem=1,
    )(*scattered(early, late, early_sends, late_sends, place))
    return (
        loss[0, 0],
        g_images,
        g_reduce[None],
        g_spatial.swapaxes(2, 3)[None],
        g_expand.T[None],
    )


def solution(mesh):
    return jax.shard_map(
        step,
        mesh=mesh,
        in_specs=(P("dp", "space", None, None), P("dp", "space", None, None), P(), P(), P(), P()),
        out_specs=(
            P(),
            P("dp", "space", None, None),
            P("dp", "space", None),
            P("dp", None, None, None, "space"),
            P("dp", None, "space"),
        ),
        check_vma=False,
    )
```
